32 devices in a mesh: groups: 2 (over x), long: 16 (over z, y, core).
Axes of the slice: x: 2, y: 2, z: 4, core: 2. Of those that a mesh axis runs over, the one named last changes fastest.
Arguments:
- displacement: float32 [4, 2, 128, 16, 256], P('groups', None, 'long'), parts along dimension 0, may hold values from -6 to 6
- velocity: float32 [4, 2, 128, 16, 256], P('groups', None, 'long'), parts along dimension 0, may hold values from -4 to 4
- damage: float32 [4, 128, 16, 256], P('groups', 'long'), parts along dimension 0, may hold values from 0 to 0.6
- material: int32 [4, 128, 16, 256], P('groups', 'long'), parts along dimension 0, may hold values from 0 to 3
- damage_table: float32 [2, 4], replicated, may hold values from 0.1 to 2
- fault_rows: int32 [4, 128, 16], P('groups', 'long'), parts along dimension 0, may hold values from 0 to 3
- kernel: float32 [16, 64, 2, 2], P(None, 'long'), may hold values from -1.5 to 1.5
- history: float32 [30, 64, 2, 2, 16], P('groups', 'long'), parts along dimension 0, may hold values from -6 to 6
Outputs:
- displacement_out: float32 [4, 2, 128, 16, 256], P('groups', None, 'long'), parts along dimension 0
- velocity_out: float32 [4, 2, 128, 16, 256], P('groups', None, 'long'), parts along dimension 0
- damage_out: float32 [4, 128, 16, 256], P('groups', 'long'), parts along dimension 0
- history_out: float32 [30, 64, 2, 2, 16], P('groups', 'long'), parts along dimension 0
The draws below stay inside these ranges and needn't reach their ends.
There are 2 independent parts, one for each index of `groups`. The reference program is written for one: setup_inputs(seed, part) draws one part's arguments, and reference() takes and returns one part's arrays. A program takes and returns all parts, laid end to end along the dimension named above; an argument that names none is the same for every part. Nothing has to cross between parts.
Inputs may be any that keep to these rules, and one draw needn't show every extreme that they name: `fault_rows`: row of the fault face, counted from the fault.
All inputs are finite; a program needn't handle non-finite values.
Results may differ from the reference program's by a relative error of at most 0.00011.
Values sent between devices are 32-bit elements; how exact they have to be, the bound alone decides.
A program may use at most 64 MiB of HBM per device.

```python
import math
import jax
import jax.numpy as jnp
from jax import lax

NY = 256
NZ = 16
COMP = 2
LAGS = 16
STEPS = 2
NCLASS = 4
FACE_ROWS = 4
NX = 128
K = 64


def touch_ends(drawn, own_key, smallest, high):
    shape = drawn.shape
    place = [jax.random.randint(jax.random.fold_in(own_key, axis), (), 0, shape[axis]) for axis in range(len(shape))]
    drawn = drawn.at[tuple(place)].set(smallest)
    longest = shape.index(max(shape))
    place[longest] = (place[longest] + 1) % shape[longest]
    return drawn.at[tuple(place)].set(high)


def levels(rng, dims, split, least, top_value):
    loudness = 1.0
    for dim, shards_of in split:
        steps = jax.random.uniform(jax.random.fold_in(jax.random.fold_in(rng, 6), dim), (shards_of,), jnp.float32, least / len(split), top_value / len(split))
        loudness = loudness * jnp.repeat(jnp.exp(steps), dims[dim] // shards_of).reshape((-1,) + (1,) * (len(dims) - 1 - dim))
    return loudness


def bell_draw(stream_key, dims, deviation, bound, pieces=(), kind=jnp.bfloat16):
    values = deviation * jax.random.normal(stream_key, dims, jnp.float32)
    if pieces:
        values = values * levels(stream_key, dims, pieces, -0.22, 0.18)
    return jnp.clip(values, -bound, bound).astype(kind)


def setup_inputs(seed: int = 0, part: int = 0) -> dict:
    key_of = jax.random.split(jax.random.key(seed), 9)
    own_keys = jax.random.split(jax.random.fold_in(key_of[8], part), 9)
    return {
        "displacement": bell_draw(own_keys[0], (COMP, 2, NX, NZ, NY), 1.0, 6.0, ((2, 16),), jnp.float32),
        "velocity": bell_draw(own_keys[1], (COMP, 2, NX, NZ, NY), 0.5, 4.0, ((2, 16),), jnp.float32),
        "damage": jnp.clip(0.6 * jax.random.uniform(own_keys[2], (2, NX, NZ, NY), jnp.float32) ** levels(own_keys[2], (2, NX, NZ, NY), ((1, 16),), -0.2, 0.2), 0.0, 0.6),
        "material": touch_ends(jax.random.randint(own_keys[3], (2, NX, NZ, NY), 0, NCLASS), jax.random.fold_in(own_keys[3], 1), 0, NCLASS - 1).astype(jnp.int32),
        "damage_table": jnp.clip(jnp.exp(jax.random.uniform(key_of[4], (2, NCLASS), jnp.float32, math.log(0.1), math.log(2.0))), 0.1, 2.0),
        "fault_rows": touch_ends(jax.random.randint(own_keys[5], (2, NX, NZ), 0, FACE_ROWS), jax.random.fold_in(own_keys[5], 1), 0, FACE_ROWS - 1).astype(jnp.int32),
        "kernel": bell_draw(key_of[6], (LAGS, K, 2, COMP), LAGS ** -0.5, 1.5, ((1, 16),), jnp.float32),
        "history": bell_draw(own_keys[7], (LAGS - 1, K, 2, COMP, NZ), 1.0, 6.0, ((1, 16),), jnp.float32),
    }


time_step = 0.5


def class_lookup(material, table_row):
    result = jnp.zeros(material.shape, table_row.dtype)
    for level in range(table_row.shape[0]):
        result = result + jnp.where(material == level, table_row[level], jnp.zeros((), table_row.dtype))
    return result


def wrap_length(values_in, axis):
    count = values_in.shape[axis]
    last_one = lax.slice_in_dim(values_in, count - 1, count, axis=axis)
    first_one = lax.slice_in_dim(values_in, 0, 1, axis=axis)
    return jnp.concatenate([last_one, values_in, first_one], axis)


def neighbour(values_in, axis, higher):
    selector = [slice(None)] * values_in.ndim
    for dimension in range(values_in.ndim - 3, values_in.ndim):
        selector[dimension] = slice(1, -1)
    selector[axis] = slice(2, None) if higher else slice(0, -2)
    return values_in[tuple(selector)]


def local_terms(padded_u, padded_c):
    outer_u = jnp.pad(padded_u, ((0, 0), (0, 0), (0, 0), (1, 1), (1, 1)))
    outer_c = jnp.pad(padded_c, ((0, 0), (0, 0), (1, 1), (1, 1)), mode="edge")
    centre_u = outer_u[:, :, 1:-1, 1:-1, 1:-1]
    centre_c = outer_c[:, 1:-1, 1:-1, 1:-1]
    forces = jnp.zeros_like(centre_u)
    energy = jnp.zeros_like(centre_c)
    for offset in range(3):
        above_u = neighbour(outer_u, 2 + offset, True)
        below_u = neighbour(outer_u, 2 + offset, False)
        above_c = neighbour(outer_c, 1 + offset, True)
        below_c = neighbour(outer_c, 1 + offset, False)
        forces = forces + (0.5 * (centre_c + above_c))[None] * (above_u - centre_u)
        forces = forces + (0.5 * (centre_c + below_c))[None] * (below_u - centre_u)
        gradient = 0.5 * (above_u - below_u)
        energy = energy + jnp.sum(gradient * gradient, axis=0)
    return forces, energy


def convolve(kernel, stacked):
    kernel_real = kernel[:, :, 0, :, None]
    kernel_imag = kernel[:, :, 1, :, None]
    spec_real = stacked[:, :, 0]
    spec_imag = stacked[:, :, 1]
    out_real = jnp.sum(kernel_real * spec_real - kernel_imag * spec_imag, axis=0)
    out_imag = jnp.sum(kernel_real * spec_imag + kernel_imag * spec_real, axis=0)
    return out_real, out_imag


def reference(displacement, velocity, damage, material, damage_table, fault_rows, kernel, history):
    rates = class_lookup(material, damage_table[0])
    limits = class_lookup(material, damage_table[1])
    heights = lax.broadcasted_iota(jnp.int32, damage.shape, 3)
    on_fault = (heights == fault_rows[..., None]).astype(displacement.dtype)
    signs = jnp.array([1.0, -1.0], displacement.dtype)[:, None, None, None]
    lagged = [history[level] for level in range(LAGS - 1)]
    for number in range(STEPS):
        stiffness = 1.0 - damage
        forces, energy = local_terms(wrap_length(displacement, 2), wrap_length(stiffness, 1))
        face = jnp.sum(displacement * on_fault[None], axis=4)
        slip = face[:, 1] - face[:, 0]
        spectrum = jnp.fft.rfft(slip, axis=1, norm="ortho")[:, :K]
        current = jnp.transpose(jnp.stack([jnp.real(spectrum), jnp.imag(spectrum)], 0), (2, 0, 1, 3))
        stacked = jnp.stack([current] + lagged, 0)
        traction_real, traction_imag = convolve(kernel, stacked)
        complete = lax.complex(traction_real, traction_imag)
        complete = jnp.concatenate([complete, jnp.zeros_like(complete[:1])], 0)
        traction = jnp.transpose(jnp.fft.irfft(complete, n=NX, axis=0, norm="ortho"), (1, 0, 2))
        pushes = traction[:, None, :, :, None] * signs[None] * on_fault[None]
        velocity = velocity + time_step * (forces + pushes)
        displacement = displacement + time_step * velocity
        damage = 1.0 - (1.0 - damage) * jnp.exp(-rates * jax.nn.softplus(energy - limits))
        lagged = [current] + lagged[:-1]
    return displacement, velocity, damage, jnp.stack(lagged, 0)
```

```python
import functools
import math

import jax
import jax.numpy as jnp
import numpy as np
from jax import lax
from jax.experimental import pallas as pl
from jax.experimental.pallas import tpu as pltpu
from jax.sharding import PartitionSpec as P

time_step = 0.5
MESH = pl.DeviceIdType.MESH
HIGHEST = lax.Precision.HIGHEST


def bases(length, cells):
    waves = np.arange(length // 2)
    places = np.arange(length)
    norming = 1.0 / math.sqrt(length)

    def table(k, x):
        phase = (k[:, None] * x[None, :] % length) * (2.0 * math.pi / length)
        return np.cos(phase) * norming, -np.sin(phase) * norming

    cosine, sine = table(waves, places)
    forward = np.stack([cosine, sine], 1).reshape(length, length)
    swapped = np.stack([sine, cosine], 1).reshape(length, length)
    cosine, sine = table(waves, np.arange(-cells, length + cells))
    weights = np.where(waves == 0, 1.0, 2.0)[:, None]
    inverse = np.stack([cosine * weights, sine * weights], 1).reshape(length, -1).T
    return np.concatenate([forward, swapped], 0).astype(np.float32), inverse.astype(np.float32)


def class_lookup(material, table_ref, row):
    count = table_ref.shape[1]
    result = jnp.full(material.shape, table_ref[row, count - 1])
    for level in range(count - 1):
        result = jnp.where(material == level, table_ref[row, level], result)
    return result


def body(
    n, disp_hbm, vel_hbm, dmg_hbm, mat_ref, table_ref, fault_ref, kr_ref, ki_ref, hist_ref,
    forward_ref, inverse_ref,
    disp_out, vel_out, dmg_out, hist_out,
    u1, u2, d1, d2, vel, face, gather1, gather2, spectra, push2,
    load_sems, halo_send, halo_recv, all_send, all_recv,
):
    cells = vel.shape[2]
    depth, rows = vel.shape[3], vel.shape[4]
    group = lax.axis_index("groups")
    me = lax.axis_index("long")
    left, right = lax.rem(me + n - 1, n), lax.rem(me + 1, n)
    dt = time_step

    barrier = pltpu.get_barrier_semaphore()

    @pl.loop(1, n)
    def _(step):
        pl.semaphore_signal(
            barrier, inc=1, device_id=(group, lax.rem(me + step, n)), device_id_type=MESH
        )

    loads = [
        pltpu.make_async_copy(disp_hbm, u1.at[:, :, pl.ds(1, cells)], load_sems.at[0]),
        pltpu.make_async_copy(dmg_hbm, d1.at[:, pl.ds(1, cells)], load_sems.at[1]),
        pltpu.make_async_copy(vel_hbm, vel, load_sems.at[2]),
    ]
    for copy in loads:
        copy.start()

    diagonal = lax.broadcasted_iota(jnp.int32, (depth, depth), 0) == lax.broadcasted_iota(
        jnp.int32, (depth, depth), 1
    )
    for s in range(2):
        rows_s = fault_ref[s].astype(jnp.float32)
        for x in range(cells):
            line = jnp.where(diagonal, rows_s[x : x + 1, :], 0.0)
            column = jnp.sum(line, axis=1, keepdims=True)
            face[s, x + 1] = jnp.broadcast_to(column, (depth, 128))

    lane = lax.broadcasted_iota(jnp.int32, (depth, 128), 1)
    lane_f = lane.astype(jnp.float32)
    lane8 = lax.broadcasted_iota(jnp.int32, (8, 128), 1)

    def slip_tile(u):
        parts = []
        for c in range(2):
            total = jnp.zeros((depth, 128), jnp.float32)
            for x in range(cells):
                on0 = jnp.where(lane_f == face[0, x + 1], u[c, 0, x + 1, :, :128], 0.0)
                on1 = jnp.where(lane_f == face[1, x + 1], u[c, 1, x + 1, :, :128], 0.0)
                column = jnp.sum(on1 - on0, axis=1, keepdims=True)
                total = jnp.where(lane == x, column, total)
            parts.append(total)
        parts.append(jnp.zeros((128 - 2 * depth, 128), jnp.float32))
        return jnp.concatenate(parts, 0).T[:cells, :]

    odd = lax.broadcasted_iota(jnp.int32, (cells, 128), 0) % 2 == 1

    def exchange(block):
        return jnp.where(odd, pltpu.roll(block, 1, 0), pltpu.roll(block, cells - 1, 0))

    lags = kr_ref.shape[0]
    sum1 = jnp.zeros((cells, 128), jnp.float32)
    sum2 = jnp.zeros((cells, 128), jnp.float32)
    for lag in range(1, lags):
        now = hist_ref[lag - 1]
        sum1 = sum1 + kr_ref[lag] * now + ki_ref[lag] * exchange(now)
        if lag >= 2:
            now = hist_ref[lag - 2]
            sum2 = sum2 + kr_ref[lag] * now + ki_ref[lag] * exchange(now)
    sum1s = exchange(sum1)

    def quarters(a, b, c, d):
        return jnp.where(
            lane8 < 32, a, jnp.where(lane8 < 64, b, jnp.where(lane8 < 96, c, d))
        )

    own = pl.ds(pl.multiple_of(me * cells, cells), cells)
    loads[0].wait()
    gather1[own, 128:256] = quarters(kr_ref[0], ki_ref[0], kr_ref[1], ki_ref[1])
    gather1[own, 0:128] = quarters(slip_tile(u1), sum1, sum1s, sum2)
    loads[1].wait()
    loads[2].wait()

    pl.semaphore_wait(barrier, n - 1)

    def to(device, source, target, index):
        return pltpu.make_async_remote_copy(
            src_ref=source, dst_ref=target, send_sem=halo_send.at[index],
            recv_sem=halo_recv.at[index], device_id=(group, device), device_id_type=MESH,
        )

    first = [
        to(left, u1.at[:, :, 1], u1.at[:, :, cells + 1], 0),
        to(right, u1.at[:, :, cells], u1.at[:, :, 0], 1),
        to(left, d1.at[:, 1], d1.at[:, cells + 1], 2),
        to(right, d1.at[:, cells], d1.at[:, 0], 3),
        to(left, face.at[:, 1], face.at[:, cells + 1], 4),
        to(right, face.at[:, cells], face.at[:, 0], 5),
    ]
    for copy in first:
        copy.start()

    def spread(buffer, index):
        @pl.loop(1, n)
        def _(step):
            pltpu.make_async_remote_copy(
                src_ref=buffer.at[own], dst_ref=buffer.at[own],
                send_sem=all_send.at[index], recv_sem=all_recv.at[index],
                device_id=(group, lax.rem(me + step, n)), device_id_type=MESH,
            ).start()

    def all_of(buffer, index):
        rest = buffer.at[pl.ds(0, (n - 1) * cells)]
        return pltpu.make_async_remote_copy(
            src_ref=rest, dst_ref=rest,
            send_sem=all_send.at[index], recv_sem=all_recv.at[index],
            device_id=(group, left), device_id_type=MESH,
        )

    spread(gather1, 0)

    zi = lax.broadcasted_iota(jnp.int32, (depth, rows), 0)
    yi = lax.broadcasted_iota(jnp.int32, (depth, rows), 1)
    ends = ((0, zi == depth - 1, depth - 1), (0, zi == 0, 1), (1, yi == rows - 1, rows - 1), (1, yi == 0, 1))

    def plane(u, d, s, x):
        here = d[s, x + 1]
        around = [d[s, x + 2], d[s, x]]
        for axis, at_end, shift in ends:
            around.append(jnp.where(at_end, here, pltpu.roll(here, shift, axis)))
        stiff = [1.0 - 0.5 * (here + other) for other in around]
        energy = None
        forces = []
        for c in range(2):
            mid = u[c, s, x + 1]
            near = [u[c, s, x + 2], u[c, s, x]]
            for axis, at_end, shift in ends:
                near.append(jnp.where(at_end, 0.0, pltpu.roll(mid, shift, axis)))
            force = stiff[0] * (near[0] - mid)
            for k in range(1, 6):
                force = force + stiff[k] * (near[k] - mid)
            forces.append(force)
            for k in range(3):
                slope = near[2 * k] - near[2 * k + 1]
                energy = slope * slope if energy is None else energy + slope * slope
        material = mat_ref[s, x]
        over = 0.25 * energy - class_lookup(material, table_ref, 1)
        soft = jnp.maximum(over, 0.0) + jnp.log(1.0 + jnp.exp(-jnp.abs(over)))
        kept = (1.0 - here) * jnp.exp(-class_lookup(material, table_ref, 0) * soft)
        return forces, 1.0 - kept

    def first_step(s, x):
        forces, damaged = plane(u1, d1, s, x)
        for c in range(2):
            speed = vel[c, s, x] + dt * forces[c]
            vel[c, s, x] = speed
            u2[c, s, x + 1] = u1[c, s, x + 1] + dt * speed
        d2[s, x + 1] = damaged

    @pl.loop(1, cells - 1)
    def _(x):
        for s in range(2):
            first_step(s, x)

    for copy in first:
        copy.wait_recv()

    @pl.loop(0, 2)
    def _(side):
        for s in range(2):
            first_step(s, side * (cells - 1))

    second = [
        to(left, u2.at[:, :, 1], u2.at[:, :, cells + 1], 6),
        to(right, u2.at[:, :, cells], u2.at[:, :, 0], 7),
        to(left, d2.at[:, 1], d2.at[:, cells + 1], 8),
        to(right, d2.at[:, cells], d2.at[:, 0], 9),
    ]
    gather2[own, :] = slip_tile(u2)
    spread(gather2, 1)
    for copy in second:
        copy.start()

    all_of(gather1, 0).wait_recv()
    waves = forward_ref.shape[0] // 2
    terms = gather1[:, 0:128]
    kernels = gather1[:, 128:256]
    spec1 = jnp.dot(forward_ref[...], terms, precision=HIGHEST, preferred_element_type=jnp.float32)
    cur, cur_s = spec1[:waves], spec1[waves:]
    kr0, ki0 = kernels, pltpu.roll(kernels, 96, 1)
    kr1, ki1 = pltpu.roll(kernels, 64, 1), pltpu.roll(kernels, 32, 1)
    tract1 = kr0 * cur + ki0 * cur_s + pltpu.roll(terms, 96, 1)
    tract1_s = kr0 * cur_s - ki0 * cur + pltpu.roll(terms, 64, 1)
    row = lax.broadcasted_iota(jnp.int32, (waves, 128), 0)
    wide = lax.broadcasted_iota(jnp.int32, (waves, 128), 1)
    back1 = 2.0 * dt * dt * jnp.where(row == 1, 0.0, tract1)
    back1_s = 2.0 * dt * dt * jnp.where(row == 0, 0.0, tract1_s)
    partial2 = kr1 * cur + ki1 * cur_s + pltpu.roll(terms, 32, 1)
    spectra[0] = cur

    all_of(gather2, 1).wait_recv()
    spec2 = jnp.dot(
        forward_ref[...], gather2[...], precision=HIGHEST, preferred_element_type=jnp.float32
    )
    cur2 = spec2[:waves] - back1
    cur2_s = spec2[waves:] - back1_s
    spectra[1] = cur2
    tract2 = kr0 * cur2 + ki0 * cur2_s + partial2
    both = jnp.where(wide < 32, tract1, jnp.where(wide < 64, pltpu.roll(tract2, 32, 1), 0.0))
    local = inverse_ref[pl.ds(pl.multiple_of(me * cells, cells), 3 * cells), :]
    traction = lax.dot_general(
        both.T, local, (((1,), (1,)), ((), ())), precision=HIGHEST,
        preferred_element_type=jnp.float32,
    )

    hist_out[0] = spectra[1, own, :]
    hist_out[1] = spectra[0, own, :]
    for lag in range(2, lags - 1):
        hist_out[lag] = hist_ref[lag - 2]

    for copy in second:
        copy.wait_recv()
        copy.wait_send()

    for x in range(cells + 2):
        for c in range(2):
            column = traction[c * depth : (c + 1) * depth, cells - 1 + x : cells + x]
            wide_column = jnp.broadcast_to(column, (depth, 128))
            for s, sign in ((0, dt), (1, -dt)):
                push = jnp.where(lane_f == face[s, x], sign * wide_column, 0.0)
                u2[c, s, x, :, :128] = u2[c, s, x, :, :128] + dt * push
                if 1 <= x <= cells:
                    vel[c, s, x - 1, :, :128] = vel[c, s, x - 1, :, :128] + push
            if 1 <= x <= cells:
                column = traction[(2 + c) * depth : (3 + c) * depth, cells - 1 + x : cells + x]
                push2[c, x - 1] = jnp.broadcast_to(dt * column, (depth, 128))

    @pl.loop(0, cells)
    def _(x):
        for s in range(2):
            forces, damaged = plane(u2, d2, s, x)
            on = lane_f == face[s, x + 1]
            for c in range(2):
                speed = vel[c, s, x] + dt * forces[c]
                push = jnp.where(on, push2[c, x], 0.0)
                near = speed[:, :128] + push if s == 0 else speed[:, :128] - push
                speed = jnp.concatenate([near, speed[:, 128:]], 1)
                vel_out[c, s, x] = speed
                disp_out[c, s, x] = u2[c, s, x + 1] + dt * speed
            dmg_out[s, x] = damaged

    for copy in first:
        copy.wait_send()
    all_of(gather1, 0).wait_send()
    all_of(gather2, 1).wait_send()


def per_device(displacement, velocity, damage, material, damage_table, fault_rows, kernel, history):
    n = lax.axis_size("long")
    parts, strips, cells, depth, rows = displacement.shape
    length = cells * n
    lags, owned = kernel.shape[0], kernel.shape[1]
    forward, inverse = bases(length, cells)

    def expanded(part):
        shape = (lags, owned, 2, 4, parts, depth)
        return jnp.broadcast_to(part[:, :, :, None, :, None], shape).reshape(lags, 2 * owned, 128)

    kr = expanded(jnp.stack([kernel[:, :, 0], kernel[:, :, 0]], 2))
    ki = expanded(jnp.stack([-kernel[:, :, 1], kernel[:, :, 1]], 2))
    hist = jnp.broadcast_to(
        history[:, :, :, None], (lags - 1, owned, 2, 4, parts, depth)
    ).reshape(lags - 1, 2 * owned, 128)
    f32 = jnp.float32
    vmem = pl.BlockSpec(memory_space=pltpu.VMEM)
    hbm = pl.BlockSpec(memory_space=pl.ANY)
    smem = pl.BlockSpec(memory_space=pltpu.SMEM)
    out = pl.pallas_call(
        functools.partial(body, n),
        out_shape=(
            jax.ShapeDtypeStruct(displacement.shape, f32),
            jax.ShapeDtypeStruct(velocity.shape, f32),
            jax.ShapeDtypeStruct(damage.shape, f32),
            jax.ShapeDtypeStruct(hist.shape, f32),
        ),
        in_specs=[hbm, hbm, hbm, vmem, smem, vmem, vmem, vmem, vmem, vmem, vmem],
        out_specs=(vmem, vmem, vmem, vmem),
        scratch_shapes=[
            pltpu.VMEM((parts, strips, cells + 2, depth, rows), f32),
            pltpu.VMEM((parts, strips, cells + 2, depth, rows), f32),
            pltpu.VMEM((strips, cells + 2, depth, rows), f32),
            pltpu.VMEM((strips, cells + 2, depth, rows), f32),
            pltpu.VMEM(velocity.shape, f32),
            pltpu.VMEM((strips, cells + 2, depth, 128), f32),
            pltpu.VMEM((length, 256), f32),
            pltpu.VMEM((length, 128), f32),
            pltpu.VMEM((2, length, 128), f32),
            pltpu.VMEM((parts, cells, depth, 128), f32),
            pltpu.SemaphoreType.DMA((3,)),
            pltpu.SemaphoreType.DMA((10,)),
            pltpu.SemaphoreType.DMA((10,)),
            pltpu.SemaphoreType.DMA((2,)),
            pltpu.SemaphoreType.DMA((2,)),
        ],
        compiler_params=pltpu.CompilerParams(
            collective_id=0, has_side_effects=True, vmem_limit_bytes=48 * 1024 * 1024
        ),
    )(
        displacement, velocity, damage, material, damage_table, fault_rows, kr, ki, hist,
        jnp.asarray(forward), jnp.asarray(inverse),
    )
    hist_new = out[3][:, :, : parts * depth].reshape(history.shape)
    return out[0], out[1], out[2], hist_new


def solution(mesh):
    placed = (
        P("groups", None, "long", None, None),
        P("groups", None, "long", None, None),
        P("groups", "long", None, None),
        P("groups", "long", None, None),
        P(),
        P("groups", "long", None),
        P(None, "long", None, None),
        P("groups", "long", None, None, None),
    )
    return jax.shard_map(
        per_device,
        mesh=mesh,
        in_specs=placed,
        out_specs=(
            P("groups", None, "long", None, None),
            P("groups", None, "long", None, None),
            P("groups", "long", None, None),
            P("groups", "long", None, None, None),
        ),
        check_vma=False,
    )
```

```python
import functools
import math

import jax
import jax.numpy as jnp
import numpy as np
from jax import lax
from jax.experimental import pallas as pl
from jax.experimental.pallas import tpu as pltpu
from jax.sharding import PartitionSpec as P

time_step = 0.5
MESH = pl.DeviceIdType.MESH
HIGHEST = lax.Precision.HIGHEST


def bases(length, cells):
    waves = np.arange(length // 2)
    places = np.arange(length)
    norming = 1.0 / math.sqrt(length)

    def table(k, x):
        phase = (k[:, None] * x[None, :] % length) * (2.0 * math.pi / length)
        return np.cos(phase) * norming, -np.sin(phase) * norming

    cosine, sine = table(waves, places)
    forward = np.stack([cosine, sine], 1).reshape(length, length)
    swapped = np.stack([sine, cosine], 1).reshape(length, length)
    cosine, sine = table(waves, np.arange(-cells, length + cells))
    weights = np.where(waves == 0, 1.0, 2.0)[:, None]
    inverse = np.stack([cosine * weights, sine * weights], 1).reshape(length, -1).T
    return np.concatenate([forward, swapped], 0).astype(np.float32), inverse.astype(np.float32)


def class_lookup(material, table_ref, row):
    count = table_ref.shape[1]
    result = jnp.full(material.shape, table_ref[row, count - 1])
    for level in range(count - 1):
        result = jnp.where(material == level, table_ref[row, level], result)
    return result


def half(lanes):
    return slice(128 * lanes, 128 * lanes + 128)


def plane(u, d, mat_ref, table_ref, s, x, h, depth):
    zi = lax.broadcasted_iota(jnp.int32, (depth, 128), 0)
    yi = lax.broadcasted_iota(jnp.int32, (depth, 128), 1)

    def nearby(ref, index, own_value, here):
        before, after = index
        near = [ref[(*after, slice(None), half(h))], ref[(*before, slice(None), half(h))]]
        end = here if own_value else 0.0
        near.append(jnp.where(zi == depth - 1, end, pltpu.roll(here, depth - 1, 0)))
        near.append(jnp.where(zi == 0, end, pltpu.roll(here, 1, 0)))
        middle = (*after[:-1], x + 1)
        other = ref[(*middle, slice(None), half(1 - h))]
        high, low = end, end
        if h == 0:
            high = pltpu.roll(other, 127, 1)
        else:
            low = pltpu.roll(other, 1, 1)
        near.append(jnp.where(yi == 127, high, pltpu.roll(here, 127, 1)))
        near.append(jnp.where(yi == 0, low, pltpu.roll(here, 1, 1)))
        return near

    here = d[s, x + 1, :, half(h)]
    stiff = [1.0 - 0.5 * (here + other) for other in nearby(d, ((s, x), (s, x + 2)), True, here)]
    energy = None
    forces = []
    for c in range(2):
        mid = u[c, s, x + 1, :, half(h)]
        near = nearby(u, ((c, s, x), (c, s, x + 2)), False, mid)
        force = stiff[0] * (near[0] - mid)
        for k in range(1, 6):
            force = force + stiff[k] * (near[k] - mid)
        forces.append(force)
        for k in range(3):
            slope = near[2 * k] - near[2 * k + 1]
            energy = slope * slope if energy is None else energy + slope * slope
    material = mat_ref[s, x, :, half(h)]
    over = 0.25 * energy - class_lookup(material, table_ref, 1)
    soft = jnp.maximum(over, 0.0) + jnp.log(1.0 + jnp.exp(-jnp.abs(over)))
    kept = (1.0 - here) * jnp.exp(-class_lookup(material, table_ref, 0) * soft)
    return forces, 1.0 - kept


def exchange_body(
    n, disp_hbm, vel_hbm, dmg_hbm, mat_ref, table_ref, fault_ref, kern_ref, hist_ref,
    forward_ref, inverse_ref,
    u2, d2, vel, face, push2, spec_out, disp_far, vel_far, dmg_far,
    u1, d1, gather1, gather2, spectra, small,
    load_sems, halo_send, halo_recv, all_send, all_recv,
):
    cells = vel.shape[2]
    depth = vel.shape[3]
    group = lax.axis_index("groups")
    me = lax.axis_index("long")
    left, right = lax.rem(me + n - 1, n), lax.rem(me + 1, n)
    dt = time_step

    barrier = pltpu.get_barrier_semaphore()

    @pl.loop(1, n)
    def _(step):
        pl.semaphore_signal(
            barrier, inc=1, device_id=(group, lax.rem(me + step, n)), device_id_type=MESH
        )

    loads = [
        pltpu.make_async_copy(disp_hbm, u1.at[:, :, pl.ds(1, cells)], load_sems.at[0]),
        pltpu.make_async_copy(dmg_hbm, d1.at[:, pl.ds(1, cells)], load_sems.at[1]),
        pltpu.make_async_copy(vel_hbm, vel, load_sems.at[2]),
    ]
    for copy in loads:
        copy.start()

    diagonal = lax.broadcasted_iota(jnp.int32, (depth, depth), 0) == lax.broadcasted_iota(
        jnp.int32, (depth, depth), 1
    )
    for s in range(2):
        rows_s = fault_ref[s].astype(jnp.float32)
        for x in range(cells):
            line = jnp.where(diagonal, rows_s[x : x + 1, :], 0.0)
            column = jnp.sum(line, axis=1, keepdims=True)
            face[s, x + 1] = jnp.broadcast_to(column, (depth, 128))

    lane = lax.broadcasted_iota(jnp.int32, (depth, 128), 1)
    lane_f = lane.astype(jnp.float32)
    lane8 = lax.broadcasted_iota(jnp.int32, (cells, 128), 1)

    def slip_tile(u):
        parts = []
        for c in range(2):
            total = jnp.zeros((depth, 128), jnp.float32)
            for x in range(cells):
                on0 = jnp.where(lane_f == face[0, x + 1], u[c, 0, x + 1, :, :128], 0.0)
                on1 = jnp.where(lane_f == face[1, x + 1], u[c, 1, x + 1, :, :128], 0.0)
                column = jnp.sum(on1 - on0, axis=1, keepdims=True)
                total = jnp.where(lane == x, column, total)
            parts.append(total)
        parts.append(jnp.zeros((128 - 2 * depth, 128), jnp.float32))
        return jnp.concatenate(parts, 0).T[:cells, :]

    odd = lax.broadcasted_iota(jnp.int32, (cells, 128), 0) % 2 == 1

    def exchange(block):
        return jnp.where(odd, pltpu.roll(block, 1, 0), pltpu.roll(block, cells - 1, 0))

    owned, lags = kern_ref.shape[0], kern_ref.shape[3]
    real, imag = kern_ref[:, 0], kern_ref[:, 1]
    at_lag = [
        [jnp.broadcast_to(part[:, :, lag : lag + 1], (owned, 2, depth)) for part in (real, imag)]
        for lag in range(lags)
    ]
    zero = jnp.zeros((owned, 2, depth), jnp.float32)
    sums = [[zero, zero], [zero, zero]]
    for lag in range(1, lags):
        kr, ki = at_lag[lag]
        for step in range(2):
            if lag - 1 - step >= 0:
                now_r, now_i = hist_ref[lag - 1 - step, :, 0], hist_ref[lag - 1 - step, :, 1]
                old_r, old_i = sums[step]
                sums[step] = [old_r + kr * now_r - ki * now_i, old_i + kr * now_i + ki * now_r]
    pairs = [
        (at_lag[0][0], at_lag[0][0]), (-at_lag[0][1], at_lag[0][1]),
        (at_lag[1][0], at_lag[1][0]), (-at_lag[1][1], at_lag[1][1]),
        sums[0], sums[1],
    ]
    small[...] = jnp.zeros_like(small)
    for q, pair in enumerate(pairs):
        for ri in range(2):
            for k in range(owned):
                for c in range(2):
                    at = c * cells + 2 * k + ri
                    small[q, at : at + 1, 0:depth] = pair[ri][k, c : c + 1, :]

    def packed(q):
        second = pltpu.roll(small[q, cells : 2 * cells], depth, 1)
        return jnp.where(lane8 < depth, small[q, 0:cells], second)

    def quarters(parts):
        a, b, c, d = [p if i == 0 else pltpu.roll(p, 32 * i, 1) for i, p in enumerate(parts)]
        return jnp.where(
            lane8 < 32, a, jnp.where(lane8 < 64, b, jnp.where(lane8 < 96, c, d))
        )

    own = pl.ds(pl.multiple_of(me * cells, cells), cells)
    gather1[own, 128:256] = quarters([packed(q) for q in range(4)])
    sum1 = packed(4)
    loads[0].wait()
    gather1[own, 0:128] = quarters([slip_tile(u1), sum1, exchange(sum1), packed(5)])
    loads[1].wait()
    loads[2].wait()

    pl.semaphore_wait(barrier, n - 1)

    def to(device, source, target, index):
        return pltpu.make_async_remote_copy(
            src_ref=source, dst_ref=target, send_sem=halo_send.at[index],
            recv_sem=halo_recv.at[index], device_id=(group, device), device_id_type=MESH,
        )

    def halo(u, d, h, index):
        lanes = pl.ds(128 * h, 128)
        everything = slice(None)
        return [
            to(left, u.at[:, :, 1, everything, lanes], u.at[:, :, cells + 1, everything, lanes], index),
            to(right, u.at[:, :, cells, everything, lanes], u.at[:, :, 0, everything, lanes], index + 1),
            to(left, d.at[:, 1, everything, lanes], d.at[:, cells + 1, everything, lanes], index + 2),
            to(right, d.at[:, cells, everything, lanes], d.at[:, 0, everything, lanes], index + 3),
        ]

    def spread(buffer, index):
        @pl.loop(1, n)
        def _(step):
            pltpu.make_async_remote_copy(
                src_ref=buffer.at[own], dst_ref=buffer.at[own],
                send_sem=all_send.at[index], recv_sem=all_recv.at[index],
                device_id=(group, lax.rem(me + step, n)), device_id_type=MESH,
            ).start()

    def all_of(buffer, index):
        rest = buffer.at[pl.ds(0, (n - 1) * cells)]
        return pltpu.make_async_remote_copy(
            src_ref=rest, dst_ref=rest,
            send_sem=all_send.at[index], recv_sem=all_recv.at[index],
            device_id=(group, left), device_id_type=MESH,
        )

    faces = [
        to(left, face.at[:, 1], face.at[:, cells + 1], 16),
        to(right, face.at[:, cells], face.at[:, 0], 17),
    ]
    near1 = halo(u1, d1, 0, 0)
    far1 = halo(u1, d1, 1, 4)
    for copy in near1:
        copy.start()
    spread(gather1, 0)
    for copy in far1 + faces:
        copy.start()

    def first_step(s, x, h):
        forces, damaged = plane(u1, d1, mat_ref, table_ref, s, x, h, depth)
        for c in range(2):
            speed = vel[c, s, x, :, half(h)] + dt * forces[c]
            vel[c, s, x, :, half(h)] = speed
            u2[c, s, x + 1, :, half(h)] = u1[c, s, x + 1, :, half(h)] + dt * speed
        d2[s, x + 1, :, half(h)] = damaged

    def step_half(h, arrivals):
        @pl.loop(1, cells - 1)
        def _(x):
            for s in range(2):
                first_step(s, x, h)

        for copy in arrivals:
            copy.wait_recv()

        @pl.loop(0, 2)
        def _(side):
            for s in range(2):
                first_step(s, side * (cells - 1), h)

    step_half(0, near1)
    gather2[own, :] = slip_tile(u2)
    spread(gather2, 1)
    near2 = halo(u2, d2, 0, 8)
    for copy in near2:
        copy.start()
    step_half(1, far1)
    far2 = halo(u2, d2, 1, 12)
    for copy in far2:
        copy.start()

    all_of(gather1, 0).wait_recv()
    waves = forward_ref.shape[0] // 2
    terms = gather1[:, 0:128]
    kernels = gather1[:, 128:256]
    spec1 = jnp.dot(forward_ref[...], terms, precision=HIGHEST, preferred_element_type=jnp.float32)
    cur, cur_s = spec1[:waves], spec1[waves:]
    kr0, ki0 = kernels, pltpu.roll(kernels, 96, 1)
    kr1, ki1 = pltpu.roll(kernels, 64, 1), pltpu.roll(kernels, 32, 1)
    tract1 = kr0 * cur + ki0 * cur_s + pltpu.roll(terms, 96, 1)
    tract1_s = kr0 * cur_s - ki0 * cur + pltpu.roll(terms, 64, 1)
    row = lax.broadcasted_iota(jnp.int32, (waves, 128), 0)
    wide = lax.broadcasted_iota(jnp.int32, (waves, 128), 1)
    back1 = 2.0 * dt * dt * jnp.where(row == 1, 0.0, tract1)
    back1_s = 2.0 * dt * dt * jnp.where(row == 0, 0.0, tract1_s)
    partial2 = kr1 * cur + ki1 * cur_s + pltpu.roll(terms, 32, 1)
    spectra[0] = cur

    for copy in near2 + far2:
        copy.wait_recv()
        copy.wait_send()

    @pl.loop(0, cells)
    def _(x):
        for s in range(2):
            forces, damaged = plane(u2, d2, mat_ref, table_ref, s, x, 1, depth)
            for c in range(2):
                speed = vel[c, s, x, :, half(1)] + dt * forces[c]
                vel_far[c, s, x] = speed
                disp_far[c, s, x] = u2[c, s, x + 1, :, half(1)] + dt * speed
            dmg_far[s, x] = damaged

    all_of(gather2, 1).wait_recv()
    spec2 = jnp.dot(
        forward_ref[...], gather2[...], precision=HIGHEST, preferred_element_type=jnp.float32
    )
    cur2 = spec2[:waves] - back1
    cur2_s = spec2[waves:] - back1_s
    spectra[1] = cur2
    tract2 = kr0 * cur2 + ki0 * cur2_s + partial2
    both = jnp.where(wide < 32, tract1, jnp.where(wide < 64, pltpu.roll(tract2, 32, 1), 0.0))
    local = inverse_ref[pl.ds(pl.multiple_of(me * cells, cells), 3 * cells), :]
    traction = lax.dot_general(
        both.T, local, (((1,), (1,)), ((), ())), precision=HIGHEST,
        preferred_element_type=jnp.float32,
    )
    spec_out[0] = spectra[1, own, :]
    spec_out[1] = spectra[0, own, :]

    for copy in faces:
        copy.wait_recv()
    for copy in faces + near1 + far1:
        copy.wait_send()

    for x in range(cells + 2):
        for c in range(2):
            column = traction[c * depth : (c + 1) * depth, cells - 1 + x : cells + x]
            wide_column = jnp.broadcast_to(column, (depth, 128))
            for s, sign in ((0, dt), (1, -dt)):
                push = jnp.where(lane_f == face[s, x], sign * wide_column, 0.0)
                u2[c, s, x, :, :128] = u2[c, s, x, :, :128] + dt * push
                if 1 <= x <= cells:
                    vel[c, s, x - 1, :, :128] = vel[c, s, x - 1, :, :128] + push
            if 1 <= x <= cells:
                column = traction[(2 + c) * depth : (3 + c) * depth, cells - 1 + x : cells + x]
                push2[c, x - 1] = jnp.broadcast_to(dt * column, (depth, 128))

    all_of(gather1, 0).wait_send()
    all_of(gather2, 1).wait_send()


def finish_body(
    u2, d2, vel, face, push2, spec, disp_far, vel_far, dmg_far, mat_ref, table_ref, hist_hbm,
    disp_out, vel_out, dmg_out, hist_out,
    disp_near, vel_near, dmg_near, newest, sems,
):
    cells, depth = vel.shape[2], vel.shape[3]
    owned = newest.shape[1]
    kept = hist_hbm.shape[0] - 2
    dt = time_step
    far = pl.ds(128, 128)
    near = pl.ds(0, 128)
    everything = slice(None)
    moves = [
        pltpu.make_async_copy(hist_hbm.at[pl.ds(0, kept)], hist_out.at[pl.ds(2, kept)], sems.at[0]),
        pltpu.make_async_copy(disp_far, disp_out.at[:, :, :, everything, far], sems.at[1]),
        pltpu.make_async_copy(vel_far, vel_out.at[:, :, :, everything, far], sems.at[2]),
        pltpu.make_async_copy(dmg_far, dmg_out.at[:, :, everything, far], sems.at[3]),
    ]
    for copy in moves:
        copy.start()
    for step in range(2):
        lines = spec[step]
        shifted = pltpu.roll(lines, 128 - depth, 1)
        for k in range(owned):
            for ri in range(2):
                at = 2 * k + ri
                newest[step, k, ri, 0:1, :] = lines[at : at + 1, 0:depth]
                newest[step, k, ri, 1:2, :] = shifted[at : at + 1, 0:depth]
    last = pltpu.make_async_copy(newest, hist_out.at[pl.ds(0, 2)], sems.at[4])
    last.start()
    lane_f = lax.broadcasted_iota(jnp.int32, (depth, 128), 1).astype(jnp.float32)

    @pl.loop(0, cells)
    def _(x):
        for s in range(2):
            forces, damaged = plane(u2, d2, mat_ref, table_ref, s, x, 0, depth)
            on = lane_f == face[s, x + 1]
            for c in range(2):
                push = jnp.where(on, push2[c, x], 0.0)
                speed = vel[c, s, x, :, half(0)] + dt * forces[c]
                speed = speed + push if s == 0 else speed - push
                vel_near[c, s, x] = speed
                disp_near[c, s, x] = u2[c, s, x + 1, :, half(0)] + dt * speed
            dmg_near[s, x] = damaged
        pltpu.make_async_copy(
            disp_near.at[:, :, x], disp_out.at[:, :, x, everything, near], sems.at[5]
        ).start()
        pltpu.make_async_copy(
            vel_near.at[:, :, x], vel_out.at[:, :, x, everything, near], sems.at[6]
        ).start()
        pltpu.make_async_copy(
            dmg_near.at[:, x], dmg_out.at[:, x, everything, near], sems.at[7]
        ).start()

    for copy in moves:
        copy.wait()
    last.wait()
    pltpu.make_async_copy(disp_near, disp_out.at[:, :, :, everything, near], sems.at[5]).wait()
    pltpu.make_async_copy(vel_near, vel_out.at[:, :, :, everything, near], sems.at[6]).wait()
    pltpu.make_async_copy(dmg_near, dmg_out.at[:, :, everything, near], sems.at[7]).wait()


def per_device(displacement, velocity, damage, material, damage_table, fault_rows, kernel, history):
    n = lax.axis_size("long")
    parts, strips, cells, depth, rows = displacement.shape
    length = cells * n
    owned = kernel.shape[1]
    forward, inverse = bases(length, cells)
    f32 = jnp.float32
    vmem = pl.BlockSpec(memory_space=pltpu.VMEM)
    hbm = pl.BlockSpec(memory_space=pltpu.HBM)
    smem = pl.BlockSpec(memory_space=pltpu.SMEM)
    narrow = (depth, 128)
    kern = jnp.transpose(kernel, (1, 2, 3, 0))
    middle = pl.pallas_call(
        functools.partial(exchange_body, n),
        out_shape=[
            jax.ShapeDtypeStruct(shape, f32)
            for shape in (
                (parts, strips, cells + 2, depth, rows),
                (strips, cells + 2, depth, rows),
                velocity.shape,
                (strips, cells + 2, *narrow),
                (parts, cells, *narrow),
                (2, cells, 128),
                (parts, strips, cells, *narrow),
                (parts, strips, cells, *narrow),
                (strips, cells, *narrow),
            )
        ],
        in_specs=[hbm, hbm, hbm, vmem, smem, vmem, vmem, vmem, vmem, vmem],
        out_specs=[vmem] * 9,
        scratch_shapes=[
            pltpu.VMEM((parts, strips, cells + 2, depth, rows), f32),
            pltpu.VMEM((strips, cells + 2, depth, rows), f32),
            pltpu.VMEM((length, 256), f32),
            pltpu.VMEM((length, 128), f32),
            pltpu.VMEM((2, length, 128), f32),
            pltpu.VMEM((6, 2 * cells, 128), f32),
            pltpu.SemaphoreType.DMA((3,)),
            pltpu.SemaphoreType.DMA((18,)),
            pltpu.SemaphoreType.DMA((18,)),
            pltpu.SemaphoreType.DMA((2,)),
            pltpu.SemaphoreType.DMA((2,)),
        ],
        compiler_params=pltpu.CompilerParams(
            collective_id=0, has_side_effects=True, vmem_limit_bytes=40 * 1024 * 1024
        ),
    )(
        displacement, velocity, damage, material, damage_table, fault_rows, kern, history,
        jnp.asarray(forward), jnp.asarray(inverse),
    )
    return pl.pallas_call(
        finish_body,
        out_shape=tuple(
            jax.ShapeDtypeStruct(a.shape, f32) for a in (displacement, velocity, damage, history)
        ),
        in_specs=[vmem] * 10 + [smem, hbm],
        out_specs=(hbm, hbm, hbm, hbm),
        scratch_shapes=[
            pltpu.VMEM((parts, strips, cells, *narrow), f32),
            pltpu.VMEM((parts, strips, cells, *narrow), f32),
            pltpu.VMEM((strips, cells, *narrow), f32),
            pltpu.VMEM((2, owned, 2, parts, depth), f32),
            pltpu.SemaphoreType.DMA((8,)),
        ],
        compiler_params=pltpu.CompilerParams(vmem_limit_bytes=24 * 1024 * 1024),
    )(*middle, material, damage_table, history)


def solution(mesh):
    placed = (
        P("groups", None, "long", None, None),
        P("groups", None, "long", None, None),
        P("groups", "long", None, None),
        P("groups", "long", None, None),
        P(),
        P("groups", "long", None),
        P(None, "long", None, None),
        P("groups", "long", None, None, None),
    )
    return jax.shard_map(
        per_device,
        mesh=mesh,
        in_specs=placed,
        out_specs=(
            P("groups", None, "long", None, None),
            P("groups", None, "long", None, None),
            P("groups", "long", None, None),
            P("groups", "long", None, None, None),
        ),
        check_vma=False,
    )
```

```python
import functools
import math

import jax
import jax.numpy as jnp
import numpy as np
from jax import lax
from jax.experimental import pallas as pl
from jax.experimental.pallas import tpu as pltpu
from jax.sharding import PartitionSpec as P

time_step = 0.5
MESH = pl.DeviceIdType.MESH
HIGHEST = lax.Precision.HIGHEST


def bases(length, cells):
    waves = np.arange(length // 2)
    places = np.arange(length)
    norming = 1.0 / math.sqrt(length)

    def table(k, x):
        phase = (k[:, None] * x[None, :] % length) * (2.0 * math.pi / length)
        return np.cos(phase) * norming, -np.sin(phase) * norming

    cosine, sine = table(waves, places)
    forward = np.stack([cosine, sine], 1).reshape(length, length)
    swapped = np.stack([sine, cosine], 1).reshape(length, length)
    cosine, sine = table(waves, np.arange(-cells, length + cells))
    weights = np.where(waves == 0, 1.0, 2.0)[:, None]
    inverse = np.stack([cosine * weights, sine * weights], 1).reshape(length, -1).T
    return np.concatenate([forward, swapped], 0).astype(np.float32), inverse.astype(np.float32)


def class_lookup(material, table_ref, row):
    count = table_ref.shape[1]
    result = jnp.full(material.shape, table_ref[row, count - 1])
    for level in range(count - 1):
        result = jnp.where(material == level, table_ref[row, level], result)
    return result


def half(lanes):
    return slice(128 * lanes, 128 * lanes + 128)


def plane(u, d, rate, limit, s, x, h, depth):
    zi = lax.broadcasted_iota(jnp.int32, (depth, 128), 0)
    yi = lax.broadcasted_iota(jnp.int32, (depth, 128), 1)

    def nearby(ref, index, own_value, here):
        before, after = index
        near = [ref[(*after, slice(None), half(h))], ref[(*before, slice(None), half(h))]]
        end = here if own_value else 0.0
        near.append(jnp.where(zi == depth - 1, end, pltpu.roll(here, depth - 1, 0)))
        near.append(jnp.where(zi == 0, end, pltpu.roll(here, 1, 0)))
        middle = (*after[:-1], x + 1)
        other = ref[(*middle, slice(None), half(1 - h))]
        high, low = end, end
        if h == 0:
            high = pltpu.roll(other, 127, 1)
        else:
            low = pltpu.roll(other, 1, 1)
        near.append(jnp.where(yi == 127, high, pltpu.roll(here, 127, 1)))
        near.append(jnp.where(yi == 0, low, pltpu.roll(here, 1, 1)))
        return near

    here = d[s, x + 1, :, half(h)]
    stiff = [1.0 - 0.5 * (here + other) for other in nearby(d, ((s, x), (s, x + 2)), True, here)]
    energy = None
    forces = []
    for c in range(2):
        mid = u[c, s, x + 1, :, half(h)]
        near = nearby(u, ((c, s, x), (c, s, x + 2)), False, mid)
        force = stiff[0] * (near[0] - mid)
        for k in range(1, 6):
            force = force + stiff[k] * (near[k] - mid)
        forces.append(force)
        for k in range(3):
            slope = near[2 * k] - near[2 * k + 1]
            energy = slope * slope if energy is None else energy + slope * slope
    over = 0.25 * energy - limit[s, x, :, half(h)]
    soft = jnp.maximum(over, 0.0) + jnp.log(1.0 + jnp.exp(-jnp.abs(over)))
    kept = (1.0 - here) * jnp.exp(-rate[s, x, :, half(h)] * soft)
    return forces, 1.0 - kept


def exchange_body(
    n, disp_hbm, vel_hbm, dmg_hbm, mat_hbm, table_hbm, fault_hbm, kern_hbm, hist_hbm,
    forward_hbm, inverse_hbm,
    u2, d2, vel, face, push2, spec_out, disp_far, vel_far, dmg_far, rate, limit,
    u1, d1, gather1, gather2, spectra, small,
    mat_ref, table_ref, fault_ref, kern_ref, hist_ref, forward_ref, inverse_ref,
    load_sems, halo_send, halo_recv, all_send, all_recv,
):
    cells = vel.shape[2]
    depth = vel.shape[3]
    group = lax.axis_index("groups")
    me = lax.axis_index("long")
    left, right = lax.rem(me + n - 1, n), lax.rem(me + 1, n)
    dt = time_step

    barrier = pltpu.get_barrier_semaphore()

    @pl.loop(1, n)
    def _(step):
        pl.semaphore_signal(
            barrier, inc=1, device_id=(group, lax.rem(me + step, n)), device_id_type=MESH
        )

    loads = [
        pltpu.make_async_copy(disp_hbm, u1.at[:, :, pl.ds(1, cells)], load_sems.at[0]),
        pltpu.make_async_copy(dmg_hbm, d1.at[:, pl.ds(1, cells)], load_sems.at[1]),
        pltpu.make_async_copy(vel_hbm, vel, load_sems.at[2]),
        pltpu.make_async_copy(fault_hbm, fault_ref, load_sems.at[3]),
        pltpu.make_async_copy(kern_hbm, kern_ref, load_sems.at[4]),
        pltpu.make_async_copy(hist_hbm, hist_ref, load_sems.at[5]),
        pltpu.make_async_copy(table_hbm, table_ref, load_sems.at[6]),
        pltpu.make_async_copy(mat_hbm, mat_ref, load_sems.at[7]),
        pltpu.make_async_copy(forward_hbm, forward_ref, load_sems.at[8]),
        pltpu.make_async_copy(inverse_hbm, inverse_ref, load_sems.at[9]),
    ]
    for k in (3, 4, 5, 0, 1, 2, 6, 7, 8, 9):
        loads[k].start()
    loads[3].wait()

    diagonal = lax.broadcasted_iota(jnp.int32, (depth, depth), 0) == lax.broadcasted_iota(
        jnp.int32, (depth, depth), 1
    )
    for s in range(2):
        rows_s = fault_ref[s].astype(jnp.float32)
        for x in range(cells):
            line = jnp.where(diagonal, rows_s[x : x + 1, :], 0.0)
            column = jnp.sum(line, axis=1, keepdims=True)
            face[s, x + 1] = jnp.broadcast_to(column, (depth, 128))

    lane = lax.broadcasted_iota(jnp.int32, (depth, 128), 1)
    lane_f = lane.astype(jnp.float32)
    lane8 = lax.broadcasted_iota(jnp.int32, (cells, 128), 1)

    def slip_tile(u):
        parts = []
        for c in range(2):
            total = jnp.zeros((depth, 128), jnp.float32)
            for x in range(cells):
                on0 = jnp.where(lane_f == face[0, x + 1], u[c, 0, x + 1, :, :128], 0.0)
                on1 = jnp.where(lane_f == face[1, x + 1], u[c, 1, x + 1, :, :128], 0.0)
                column = jnp.sum(on1 - on0, axis=1, keepdims=True)
                total = jnp.where(lane == x, column, total)
            parts.append(total)
        parts.append(jnp.zeros((128 - 2 * depth, 128), jnp.float32))
        return jnp.concatenate(parts, 0).T[:cells, :]

    odd = lax.broadcasted_iota(jnp.int32, (cells, 128), 0) % 2 == 1

    def exchange(block):
        return jnp.where(odd, pltpu.roll(block, 1, 0), pltpu.roll(block, cells - 1, 0))

    loads[4].wait()
    loads[5].wait()
    owned, lags = kern_ref.shape[0], kern_ref.shape[3]
    real, imag = kern_ref[:, 0], kern_ref[:, 1]
    at_lag = [
        [jnp.broadcast_to(part[:, :, lag : lag + 1], (owned, 2, depth)) for part in (real, imag)]
        for lag in range(lags)
    ]
    zero = jnp.zeros((owned, 2, depth), jnp.float32)
    sums = [[zero, zero], [zero, zero]]
    for lag in range(1, lags):
        kr, ki = at_lag[lag]
        for step in range(2):
            if lag - 1 - step >= 0:
                now_r, now_i = hist_ref[lag - 1 - step, :, 0], hist_ref[lag - 1 - step, :, 1]
                old_r, old_i = sums[step]
                sums[step] = [old_r + kr * now_r - ki * now_i, old_i + kr * now_i + ki * now_r]
    pairs = [
        (at_lag[0][0], at_lag[0][0]), (-at_lag[0][1], at_lag[0][1]),
        (at_lag[1][0], at_lag[1][0]), (-at_lag[1][1], at_lag[1][1]),
        sums[0], sums[1],
    ]
    small[...] = jnp.zeros_like(small)
    for q, pair in enumerate(pairs):
        for ri in range(2):
            for k in range(owned):
                for c in range(2):
                    at = c * cells + 2 * k + ri
                    small[q, at : at + 1, 0:depth] = pair[ri][k, c : c + 1, :]

    def packed(q):
        second = pltpu.roll(small[q, cells : 2 * cells], depth, 1)
        return jnp.where(lane8 < depth, small[q, 0:cells], second)

    def quarters(parts):
        a, b, c, d = [p if i == 0 else pltpu.roll(p, 32 * i, 1) for i, p in enumerate(parts)]
        return jnp.where(
            lane8 < 32, a, jnp.where(lane8 < 64, b, jnp.where(lane8 < 96, c, d))
        )

    own = pl.ds(pl.multiple_of(me * cells, cells), cells)
    gather1[own, 128:256] = quarters([packed(q) for q in range(4)])
    sum1 = packed(4)
    loads[0].wait()
    gather1[own, 0:128] = quarters([slip_tile(u1), sum1, exchange(sum1), packed(5)])
    loads[1].wait()

    pl.semaphore_wait(barrier, n - 1)

    def to(device, source, target, index):
        return pltpu.make_async_remote_copy(
            src_ref=source, dst_ref=target, send_sem=halo_send.at[index],
            recv_sem=halo_recv.at[index], device_id=(group, device), device_id_type=MESH,
        )

    def halo(u, d, h, index):
        lanes = pl.ds(128 * h, 128)
        everything = slice(None)
        return [
            to(left, u.at[:, :, 1, everything, lanes], u.at[:, :, cells + 1, everything, lanes], index),
            to(right, u.at[:, :, cells, everything, lanes], u.at[:, :, 0, everything, lanes], index + 1),
            to(left, d.at[:, 1, everything, lanes], d.at[:, cells + 1, everything, lanes], index + 2),
            to(right, d.at[:, cells, everything, lanes], d.at[:, 0, everything, lanes], index + 3),
        ]

    def spread(buffer, index):
        @pl.loop(1, n)
        def _(step):
            pltpu.make_async_remote_copy(
                src_ref=buffer.at[own], dst_ref=buffer.at[own],
                send_sem=all_send.at[index], recv_sem=all_recv.at[index],
                device_id=(group, lax.rem(me + step, n)), device_id_type=MESH,
            ).start()

    def all_of(buffer, index):
        rest = buffer.at[pl.ds(0, (n - 1) * cells)]
        return pltpu.make_async_remote_copy(
            src_ref=rest, dst_ref=rest,
            send_sem=all_send.at[index], recv_sem=all_recv.at[index],
            device_id=(group, left), device_id_type=MESH,
        )

    faces = [
        to(left, face.at[:, 1], face.at[:, cells + 1], 16),
        to(right, face.at[:, cells], face.at[:, 0], 17),
    ]
    near1 = halo(u1, d1, 0, 0)
    far1 = halo(u1, d1, 1, 4)
    for copy in near1:
        copy.start()
    spread(gather1, 0)
    for copy in far1 + faces:
        copy.start()
    for k in (2, 6, 7, 8, 9):
        loads[k].wait()

    def first_step(s, x, h):
        material = mat_ref[s, x, :, half(h)]
        rate[s, x, :, half(h)] = class_lookup(material, table_ref, 0)
        limit[s, x, :, half(h)] = class_lookup(material, table_ref, 1)
        forces, damaged = plane(u1, d1, rate, limit, s, x, h, depth)
        for c in range(2):
            speed = vel[c, s, x, :, half(h)] + dt * forces[c]
            vel[c, s, x, :, half(h)] = speed
            u2[c, s, x + 1, :, half(h)] = u1[c, s, x + 1, :, half(h)] + dt * speed
        d2[s, x + 1, :, half(h)] = damaged

    def step_half(h, arrivals):
        @pl.loop(1, cells - 1)
        def _(x):
            for s in range(2):
                first_step(s, x, h)

        for copy in arrivals:
            copy.wait_recv()

        @pl.loop(0, 2)
        def _(side):
            for s in range(2):
                first_step(s, side * (cells - 1), h)

    step_half(0, near1)
    gather2[own, :] = slip_tile(u2)
    spread(gather2, 1)
    near2 = halo(u2, d2, 0, 8)
    for copy in near2:
        copy.start()
    step_half(1, far1)
    far2 = halo(u2, d2, 1, 12)
    for copy in far2:
        copy.start()

    all_of(gather1, 0).wait_recv()
    waves = forward_ref.shape[0] // 2
    terms = gather1[:, 0:128]
    kernels = gather1[:, 128:256]
    spec1 = jnp.dot(forward_ref[...], terms, precision=HIGHEST, preferred_element_type=jnp.float32)
    cur, cur_s = spec1[:waves], spec1[waves:]
    kr0, ki0 = kernels, pltpu.roll(kernels, 96, 1)
    kr1, ki1 = pltpu.roll(kernels, 64, 1), pltpu.roll(kernels, 32, 1)
    tract1 = kr0 * cur + ki0 * cur_s + pltpu.roll(terms, 96, 1)
    tract1_s = kr0 * cur_s - ki0 * cur + pltpu.roll(terms, 64, 1)
    row = lax.broadcasted_iota(jnp.int32, (waves, 128), 0)
    wide = lax.broadcasted_iota(jnp.int32, (waves, 128), 1)
    back1 = 2.0 * dt * dt * jnp.where(row == 1, 0.0, tract1)
    back1_s = 2.0 * dt * dt * jnp.where(row == 0, 0.0, tract1_s)
    partial2 = kr1 * cur + ki1 * cur_s + pltpu.roll(terms, 32, 1)
    spectra[0] = cur

    for copy in near2 + far2:
        copy.wait_recv()
        copy.wait_send()

    @pl.loop(0, cells)
    def _(x):
        for s in range(2):
            forces, damaged = plane(u2, d2, rate, limit, s, x, 1, depth)
            for c in range(2):
                speed = vel[c, s, x, :, half(1)] + dt * forces[c]
                vel_far[c, s, x] = speed
                disp_far[c, s, x] = u2[c, s, x + 1, :, half(1)] + dt * speed
            dmg_far[s, x] = damaged

    all_of(gather2, 1).wait_recv()
    spec2 = jnp.dot(
        forward_ref[...], gather2[...], precision=HIGHEST, preferred_element_type=jnp.float32
    )
    cur2 = spec2[:waves] - back1
    cur2_s = spec2[waves:] - back1_s
    spectra[1] = cur2
    tract2 = kr0 * cur2 + ki0 * cur2_s + partial2
    both = jnp.where(wide < 32, tract1, jnp.where(wide < 64, pltpu.roll(tract2, 32, 1), 0.0))
    local = inverse_ref[pl.ds(pl.multiple_of(me * cells, cells), 3 * cells), :]
    traction = lax.dot_general(
        both.T, local, (((1,), (1,)), ((), ())), precision=HIGHEST,
        preferred_element_type=jnp.float32,
    )
    spec_out[0] = spectra[1, own, :]
    spec_out[1] = spectra[0, own, :]

    for copy in faces:
        copy.wait_recv()
    for copy in faces + near1 + far1:
        copy.wait_send()

    for x in range(cells + 2):
        for c in range(2):
            column = traction[c * depth : (c + 1) * depth, cells - 1 + x : cells + x]
            wide_column = jnp.broadcast_to(column, (depth, 128))
            for s, sign in ((0, dt), (1, -dt)):
                push = jnp.where(lane_f == face[s, x], sign * wide_column, 0.0)
                u2[c, s, x, :, :128] = u2[c, s, x, :, :128] + dt * push
                if 1 <= x <= cells:
                    vel[c, s, x - 1, :, :128] = vel[c, s, x - 1, :, :128] + push
            if 1 <= x <= cells:
                column = traction[(2 + c) * depth : (3 + c) * depth, cells - 1 + x : cells + x]
                push2[c, x - 1] = jnp.broadcast_to(dt * column, (depth, 128))

    all_of(gather1, 0).wait_send()
    all_of(gather2, 1).wait_send()


def finish_body(
    u2, d2, vel, face, push2, spec, disp_far, vel_far, dmg_far, rate, limit, hist_hbm,
    disp_out, vel_out, dmg_out, hist_out,
    disp_near, vel_near, dmg_near, newest, sems,
):
    cells, depth = vel.shape[2], vel.shape[3]
    owned = newest.shape[1]
    kept = hist_hbm.shape[0] - 2
    dt = time_step
    far = pl.ds(128, 128)
    near = pl.ds(0, 128)
    everything = slice(None)
    moves = [
        pltpu.make_async_copy(hist_hbm.at[pl.ds(0, kept)], hist_out.at[pl.ds(2, kept)], sems.at[0]),
        pltpu.make_async_copy(disp_far, disp_out.at[:, :, :, everything, far], sems.at[1]),
        pltpu.make_async_copy(vel_far, vel_out.at[:, :, :, everything, far], sems.at[2]),
        pltpu.make_async_copy(dmg_far, dmg_out.at[:, :, everything, far], sems.at[3]),
    ]
    for copy in moves:
        copy.start()
    for step in range(2):
        lines = spec[step]
        shifted = pltpu.roll(lines, 128 - depth, 1)
        for k in range(owned):
            for ri in range(2):
                at = 2 * k + ri
                newest[step, k, ri, 0:1, :] = lines[at : at + 1, 0:depth]
                newest[step, k, ri, 1:2, :] = shifted[at : at + 1, 0:depth]
    last = pltpu.make_async_copy(newest, hist_out.at[pl.ds(0, 2)], sems.at[4])
    last.start()
    lane_f = lax.broadcasted_iota(jnp.int32, (depth, 128), 1).astype(jnp.float32)

    @pl.loop(0, cells)
    def _(x):
        for s in range(2):
            forces, damaged = plane(u2, d2, rate, limit, s, x, 0, depth)
            on = lane_f == face[s, x + 1]
            for c in range(2):
                push = jnp.where(on, push2[c, x], 0.0)
                speed = vel[c, s, x, :, half(0)] + dt * forces[c]
                speed = speed + push if s == 0 else speed - push
                vel_near[c, s, x] = speed
                disp_near[c, s, x] = u2[c, s, x + 1, :, half(0)] + dt * speed
            dmg_near[s, x] = damaged
        pltpu.make_async_copy(
            disp_near.at[:, :, x], disp_out.at[:, :, x, everything, near], sems.at[5]
        ).start()
        pltpu.make_async_copy(
            vel_near.at[:, :, x], vel_out.at[:, :, x, everything, near], sems.at[6]
        ).start()
        pltpu.make_async_copy(
            dmg_near.at[:, x], dmg_out.at[:, x, everything, near], sems.at[7]
        ).start()

    for copy in moves:
        copy.wait()
    last.wait()
    pltpu.make_async_copy(disp_near, disp_out.at[:, :, :, everything, near], sems.at[5]).wait()
    pltpu.make_async_copy(vel_near, vel_out.at[:, :, :, everything, near], sems.at[6]).wait()
    pltpu.make_async_copy(dmg_near, dmg_out.at[:, :, everything, near], sems.at[7]).wait()


def per_device(displacement, velocity, damage, material, damage_table, fault_rows, kernel, history):
    n = lax.axis_size("long")
    parts, strips, cells, depth, rows = displacement.shape
    length = cells * n
    owned = kernel.shape[1]
    forward, inverse = bases(length, cells)
    f32 = jnp.float32
    vmem = pl.BlockSpec(memory_space=pltpu.VMEM)
    hbm = pl.BlockSpec(memory_space=pltpu.HBM)

    def held(array):
        return pltpu.with_memory_space_constraint(array, pltpu.HBM)

    narrow = (depth, 128)
    kern = jnp.transpose(kernel, (1, 2, 3, 0))
    middle = pl.pallas_call(
        functools.partial(exchange_body, n),
        out_shape=[
            pltpu.VMEM(shape, f32)
            for shape in (
                (parts, strips, cells + 2, depth, rows),
                (strips, cells + 2, depth, rows),
                velocity.shape,
                (strips, cells + 2, *narrow),
                (parts, cells, *narrow),
                (2, cells, 128),
                (parts, strips, cells, *narrow),
                (parts, strips, cells, *narrow),
                (strips, cells, *narrow),
                damage.shape,
                damage.shape,
            )
        ],
        in_specs=[hbm] * 10,
        out_specs=[vmem] * 11,
        scratch_shapes=[
            pltpu.VMEM((parts, strips, cells + 2, depth, rows), f32),
            pltpu.VMEM((strips, cells + 2, depth, rows), f32),
            pltpu.VMEM((length, 256), f32),
            pltpu.VMEM((length, 128), f32),
            pltpu.VMEM((2, length, 128), f32),
            pltpu.VMEM((6, 2 * cells, 128), f32),
            pltpu.VMEM(material.shape, material.dtype),
            pltpu.SMEM(damage_table.shape, f32),
            pltpu.VMEM(fault_rows.shape, fault_rows.dtype),
            pltpu.VMEM(kern.shape, f32),
            pltpu.VMEM(history.shape, f32),
            pltpu.VMEM(forward.shape, f32),
            pltpu.VMEM(inverse.shape, f32),
            pltpu.SemaphoreType.DMA((10,)),
            pltpu.SemaphoreType.DMA((18,)),
            pltpu.SemaphoreType.DMA((18,)),
            pltpu.SemaphoreType.DMA((2,)),
            pltpu.SemaphoreType.DMA((2,)),
        ],
        compiler_params=pltpu.CompilerParams(
            collective_id=0, has_side_effects=True, vmem_limit_bytes=40 * 1024 * 1024
        ),
    )(
        *map(held, (
            displacement, velocity, damage, material, damage_table, fault_rows, kern, history,
            jnp.asarray(forward), jnp.asarray(inverse),
        ))
    )
    return pl.pallas_call(
        finish_body,
        out_shape=tuple(
            jax.ShapeDtypeStruct(a.shape, f32) for a in (displacement, velocity, damage, history)
        ),
        in_specs=[vmem] * 11 + [hbm],
        out_specs=(hbm, hbm, hbm, hbm),
        scratch_shapes=[
            pltpu.VMEM((parts, strips, cells, *narrow), f32),
            pltpu.VMEM((parts, strips, cells, *narrow), f32),
            pltpu.VMEM((strips, cells, *narrow), f32),
            pltpu.VMEM((2, owned, 2, parts, depth), f32),
            pltpu.SemaphoreType.DMA((8,)),
        ],
        compiler_params=pltpu.CompilerParams(vmem_limit_bytes=24 * 1024 * 1024),
    )(*middle, held(history))


def solution(mesh):
    placed = (
        P("groups", None, "long", None, None),
        P("groups", None, "long", None, None),
        P("groups", "long", None, None),
        P("groups", "long", None, None),
        P(),
        P("groups", "long", None),
        P(None, "long", None, None),
        P("groups", "long", None, None, None),
    )
    return jax.shard_map(
        per_device,
        mesh=mesh,
        in_specs=placed,
        out_specs=(
            P("groups", None, "long", None, None),
            P("groups", None, "long", None, None),
            P("groups", "long", None, None),
            P("groups", "long", None, None, None),
        ),
        check_vma=False,
    )
```

```python
import functools
import math

import jax
import jax.numpy as jnp
import numpy as np
from jax import lax
from jax.experimental import pallas as pl
from jax.experimental.pallas import tpu as pltpu
from jax.sharding import PartitionSpec as P

time_step = 0.5
MESH = pl.DeviceIdType.MESH
HIGHEST = lax.Precision.HIGHEST


def bases(length, cells):
    waves = np.arange(length // 2)
    places = np.arange(length)
    norming = 1.0 / math.sqrt(length)

    def table(k, x):
        phase = (k[:, None] * x[None, :] % length) * (2.0 * math.pi / length)
        return np.cos(phase) * norming, -np.sin(phase) * norming

    cosine, sine = table(waves, places)
    forward = np.stack([cosine, sine], 1).reshape(length, length)
    swapped = np.stack([sine, cosine], 1).reshape(length, length)
    cosine, sine = table(waves, np.arange(-cells, length + cells))
    weights = np.where(waves == 0, 1.0, 2.0)[:, None]
    inverse = np.stack([cosine * weights, sine * weights], 1).reshape(length, -1).T
    return np.concatenate([forward, swapped], 0).astype(np.float32), inverse.astype(np.float32)


def class_lookup(material, table_ref, row):
    count = table_ref.shape[1]
    result = jnp.full(material.shape, table_ref[row, count - 1])
    for level in range(count - 1):
        result = jnp.where(material == level, table_ref[row, level], result)
    return result


def half(lanes):
    return slice(128 * lanes, 128 * lanes + 128)


def plane(u, d, rate, limit, s, x, h, depth):
    zi = lax.broadcasted_iota(jnp.int32, (depth, 128), 0)
    yi = lax.broadcasted_iota(jnp.int32, (depth, 128), 1)

    def nearby(ref, index, own_value, here):
        before, after = index
        near = [ref[(*after, slice(None), half(h))], ref[(*before, slice(None), half(h))]]
        end = here if own_value else 0.0
        near.append(jnp.where(zi == depth - 1, end, pltpu.roll(here, depth - 1, 0)))
        near.append(jnp.where(zi == 0, end, pltpu.roll(here, 1, 0)))
        middle = (*after[:-1], x + 1)
        other = ref[(*middle, slice(None), half(1 - h))]
        high, low = end, end
        if h == 0:
            high = pltpu.roll(other, 127, 1)
        else:
            low = pltpu.roll(other, 1, 1)
        near.append(jnp.where(yi == 127, high, pltpu.roll(here, 127, 1)))
        near.append(jnp.where(yi == 0, low, pltpu.roll(here, 1, 1)))
        return near

    here = d[s, x + 1, :, half(h)]
    stiff = [1.0 - 0.5 * (here + other) for other in nearby(d, ((s, x), (s, x + 2)), True, here)]
    energy = None
    forces = []
    for c in range(2):
        mid = u[c, s, x + 1, :, half(h)]
        near = nearby(u, ((c, s, x), (c, s, x + 2)), False, mid)
        force = stiff[0] * (near[0] - mid)
        for k in range(1, 6):
            force = force + stiff[k] * (near[k] - mid)
        forces.append(force)
        for k in range(3):
            slope = near[2 * k] - near[2 * k + 1]
            energy = slope * slope if energy is None else energy + slope * slope
    over = 0.25 * energy - limit[s, x, :, half(h)]
    soft = jnp.maximum(over, 0.0) + jnp.log(1.0 + jnp.exp(-jnp.abs(over)))
    kept = (1.0 - here) * jnp.exp(-rate[s, x, :, half(h)] * soft)
    return forces, 1.0 - kept


def exchange_body(
    n, disp_hbm, vel_hbm, dmg_hbm, mat_hbm, table_hbm, fault_hbm, kern_hbm, hist_hbm,
    forward_hbm, inverse_hbm,
    u2, d2, vel, face, push2, spec_out, disp_far, vel_far, dmg_far, rate, limit, hist_ref,
    u1, d1, gather1, gather2, spectra, small,
    mat_ref, table_ref, fault_ref, kern_ref, forward_ref, inverse_ref,
    load_sems, halo_send, halo_recv, all_send, all_recv,
):
    cells = vel.shape[2]
    depth = vel.shape[3]
    group = lax.axis_index("groups")
    me = lax.axis_index("long")
    left, right = lax.rem(me + n - 1, n), lax.rem(me + 1, n)
    dt = time_step

    barrier = pltpu.get_barrier_semaphore()

    @pl.loop(1, n)
    def _(step):
        pl.semaphore_signal(
            barrier, inc=1, device_id=(group, lax.rem(me + step, n)), device_id_type=MESH
        )

    loads = [
        pltpu.make_async_copy(disp_hbm, u1.at[:, :, pl.ds(1, cells)], load_sems.at[0]),
        pltpu.make_async_copy(dmg_hbm, d1.at[:, pl.ds(1, cells)], load_sems.at[1]),
        pltpu.make_async_copy(vel_hbm, vel, load_sems.at[2]),
        pltpu.make_async_copy(fault_hbm, fault_ref, load_sems.at[3]),
        pltpu.make_async_copy(kern_hbm, kern_ref, load_sems.at[4]),
        pltpu.make_async_copy(hist_hbm, hist_ref, load_sems.at[5]),
        pltpu.make_async_copy(table_hbm, table_ref, load_sems.at[6]),
        pltpu.make_async_copy(mat_hbm, mat_ref, load_sems.at[7]),
        pltpu.make_async_copy(forward_hbm, forward_ref, load_sems.at[8]),
        pltpu.make_async_copy(inverse_hbm, inverse_ref, load_sems.at[9]),
    ]
    for k in (3, 6, 0, 1, 2, 7, 4, 5, 8, 9):
        loads[k].start()
    pl.semaphore_wait(barrier, n - 1)

    def to(device, source, target, index):
        return pltpu.make_async_remote_copy(
            src_ref=source, dst_ref=target, send_sem=halo_send.at[index],
            recv_sem=halo_recv.at[index], device_id=(group, device), device_id_type=MESH,
        )

    def halo(u_from, d_from, low, u, d, h, index):
        lanes = pl.ds(128 * h, 128)
        everything = slice(None)
        high = low + cells - 1
        return [
            to(left, u_from.at[:, :, low, everything, lanes], u.at[:, :, cells + 1, everything, lanes], index),
            to(right, u_from.at[:, :, high, everything, lanes], u.at[:, :, 0, everything, lanes], index + 1),
            to(left, d_from.at[:, low, everything, lanes], d.at[:, cells + 1, everything, lanes], index + 2),
            to(right, d_from.at[:, high, everything, lanes], d.at[:, 0, everything, lanes], index + 3),
        ]

    own = pl.ds(pl.multiple_of(me * cells, cells), cells)

    def spread(buffer, index):
        @pl.loop(1, n)
        def _(step):
            pltpu.make_async_remote_copy(
                src_ref=buffer.at[own], dst_ref=buffer.at[own],
                send_sem=all_send.at[index], recv_sem=all_recv.at[index],
                device_id=(group, lax.rem(me + step, n)), device_id_type=MESH,
            ).start()

    def all_of(buffer, index):
        rest = buffer.at[pl.ds(0, (n - 1) * cells)]
        return pltpu.make_async_remote_copy(
            src_ref=rest, dst_ref=rest,
            send_sem=all_send.at[index], recv_sem=all_recv.at[index],
            device_id=(group, left), device_id_type=MESH,
        )

    faces = [
        to(left, face.at[:, 1], face.at[:, cells + 1], 16),
        to(right, face.at[:, cells], face.at[:, 0], 17),
    ]
    near1 = halo(disp_hbm, dmg_hbm, 0, u1, d1, 0, 0)
    far1 = halo(disp_hbm, dmg_hbm, 0, u1, d1, 1, 4)
    for copy in near1 + far1:
        copy.start()
    loads[3].wait()

    diagonal = lax.broadcasted_iota(jnp.int32, (depth, depth), 0) == lax.broadcasted_iota(
        jnp.int32, (depth, depth), 1
    )
    for s in range(2):
        rows_s = fault_ref[s].astype(jnp.float32)
        for x in range(cells):
            line = jnp.where(diagonal, rows_s[x : x + 1, :], 0.0)
            column = jnp.sum(line, axis=1, keepdims=True)
            face[s, x + 1] = jnp.broadcast_to(column, (depth, 128))

    lane = lax.broadcasted_iota(jnp.int32, (depth, 128), 1)
    lane_f = lane.astype(jnp.float32)
    lane8 = lax.broadcasted_iota(jnp.int32, (cells, 128), 1)

    def slip_tile(u):
        parts = []
        for c in range(2):
            total = jnp.zeros((depth, 128), jnp.float32)
            for x in range(cells):
                on0 = jnp.where(lane_f == face[0, x + 1], u[c, 0, x + 1, :, :128], 0.0)
                on1 = jnp.where(lane_f == face[1, x + 1], u[c, 1, x + 1, :, :128], 0.0)
                column = jnp.sum(on1 - on0, axis=1, keepdims=True)
                total = jnp.where(lane == x, column, total)
            parts.append(total)
        parts.append(jnp.zeros((128 - 2 * depth, 128), jnp.float32))
        return jnp.concatenate(parts, 0).T[:cells, :]

    for copy in faces:
        copy.start()
    for k in (0, 1, 2, 6, 7):
        loads[k].wait()

    def first_step(s, x, h):
        material = mat_ref[s, x, :, half(h)]
        rate[s, x, :, half(h)] = class_lookup(material, table_ref, 0)
        limit[s, x, :, half(h)] = class_lookup(material, table_ref, 1)
        forces, damaged = plane(u1, d1, rate, limit, s, x, h, depth)
        for c in range(2):
            speed = vel[c, s, x, :, half(h)] + dt * forces[c]
            vel[c, s, x, :, half(h)] = speed
            u2[c, s, x + 1, :, half(h)] = u1[c, s, x + 1, :, half(h)] + dt * speed
        d2[s, x + 1, :, half(h)] = damaged

    def step_half(h, arrivals):
        @pl.loop(0, cells // 2 - 1)
        def _(pair):
            for x in (2 * pair + 1, 2 * pair + 2):
                for s in range(2):
                    first_step(s, x, h)

        for copy in arrivals:
            copy.wait_recv()

        for x in (0, cells - 1):
            for s in range(2):
                first_step(s, x, h)

    step_half(0, near1)
    gather2[own, :] = slip_tile(u2)
    spread(gather2, 1)
    near2 = halo(u2, d2, 1, u2, d2, 0, 8)
    for copy in near2:
        copy.start()
    odd = lax.broadcasted_iota(jnp.int32, (cells, 128), 0) % 2 == 1

    def exchange(block):
        return jnp.where(odd, pltpu.roll(block, 1, 0), pltpu.roll(block, cells - 1, 0))

    loads[4].wait()
    loads[5].wait()
    owned, lags = kern_ref.shape[0], kern_ref.shape[3]
    real, imag = kern_ref[:, 0], kern_ref[:, 1]
    at_lag = [
        [jnp.broadcast_to(part[:, :, lag : lag + 1], (owned, 2, depth)) for part in (real, imag)]
        for lag in range(lags)
    ]
    zero = jnp.zeros((owned, 2, depth), jnp.float32)
    sums = [[zero, zero], [zero, zero]]
    for lag in range(1, lags):
        kr, ki = at_lag[lag]
        for step in range(2):
            if lag - 1 - step >= 0:
                now_r, now_i = hist_ref[lag - 1 - step, :, 0], hist_ref[lag - 1 - step, :, 1]
                old_r, old_i = sums[step]
                sums[step] = [old_r + kr * now_r - ki * now_i, old_i + kr * now_i + ki * now_r]
    pairs = [
        (at_lag[0][0], at_lag[0][0]), (-at_lag[0][1], at_lag[0][1]),
        (at_lag[1][0], at_lag[1][0]), (-at_lag[1][1], at_lag[1][1]),
        sums[0], sums[1],
    ]
    small[...] = jnp.zeros_like(small)
    for q, pair in enumerate(pairs):
        for ri in range(2):
            for k in range(owned):
                for c in range(2):
                    at = c * cells + 2 * k + ri
                    small[q, at : at + 1, 0:depth] = pair[ri][k, c : c + 1, :]

    def packed(q):
        second = pltpu.roll(small[q, cells : 2 * cells], depth, 1)
        return jnp.where(lane8 < depth, small[q, 0:cells], second)

    def quarters(parts):
        a, b, c, d = [p if i == 0 else pltpu.roll(p, 32 * i, 1) for i, p in enumerate(parts)]
        return jnp.where(
            lane8 < 32, a, jnp.where(lane8 < 64, b, jnp.where(lane8 < 96, c, d))
        )

    gather1[own, 128:256] = quarters([packed(q) for q in range(4)])
    sum1 = packed(4)
    gather1[own, 0:128] = quarters([slip_tile(u1), sum1, exchange(sum1), packed(5)])

    spread(gather1, 0)
    step_half(1, far1)
    far2 = halo(u2, d2, 1, u2, d2, 1, 12)
    for copy in far2:
        copy.start()

    loads[8].wait()
    loads[9].wait()
    all_of(gather1, 0).wait_recv()
    waves = forward_ref.shape[0] // 2
    terms = gather1[:, 0:128]
    kernels = gather1[:, 128:256]
    spec1 = jnp.dot(forward_ref[...], terms, precision=HIGHEST, preferred_element_type=jnp.float32)
    cur, cur_s = spec1[:waves], spec1[waves:]
    kr0, ki0 = kernels, pltpu.roll(kernels, 96, 1)
    kr1, ki1 = pltpu.roll(kernels, 64, 1), pltpu.roll(kernels, 32, 1)
    tract1 = kr0 * cur + ki0 * cur_s + pltpu.roll(terms, 96, 1)
    tract1_s = kr0 * cur_s - ki0 * cur + pltpu.roll(terms, 64, 1)
    row = lax.broadcasted_iota(jnp.int32, (waves, 128), 0)
    wide = lax.broadcasted_iota(jnp.int32, (waves, 128), 1)
    back1 = 2.0 * dt * dt * jnp.where(row == 1, 0.0, tract1)
    back1_s = 2.0 * dt * dt * jnp.where(row == 0, 0.0, tract1_s)
    partial2 = kr1 * cur + ki1 * cur_s + pltpu.roll(terms, 32, 1)
    spectra[0] = cur

    for copy in near2 + far2:
        copy.wait_recv()
        copy.wait_send()

    @pl.loop(0, cells // 2)
    def _(pair):
        for x in (2 * pair, 2 * pair + 1):
            for s in range(2):
                forces, damaged = plane(u2, d2, rate, limit, s, x, 1, depth)
                for c in range(2):
                    speed = vel[c, s, x, :, half(1)] + dt * forces[c]
                    vel_far[c, s, x] = speed
                    disp_far[c, s, x] = u2[c, s, x + 1, :, half(1)] + dt * speed
                dmg_far[s, x] = damaged

    all_of(gather2, 1).wait_recv()
    spec2 = jnp.dot(
        forward_ref[...], gather2[...], precision=HIGHEST, preferred_element_type=jnp.float32
    )
    cur2 = spec2[:waves] - back1
    cur2_s = spec2[waves:] - back1_s
    spectra[1] = cur2
    tract2 = kr0 * cur2 + ki0 * cur2_s + partial2
    both = jnp.where(wide < 32, tract1, jnp.where(wide < 64, pltpu.roll(tract2, 32, 1), 0.0))
    local = inverse_ref[pl.ds(pl.multiple_of(me * cells, cells), 3 * cells), :]
    traction = lax.dot_general(
        both.T, local, (((1,), (1,)), ((), ())), precision=HIGHEST,
        preferred_element_type=jnp.float32,
    )
    spec_out[0] = spectra[1, own, :]
    spec_out[1] = spectra[0, own, :]

    for copy in faces:
        copy.wait_recv()
    for copy in faces + near1 + far1:
        copy.wait_send()

    for x in range(cells + 2):
        for c in range(2):
            column = traction[c * depth : (c + 1) * depth, cells - 1 + x : cells + x]
            wide_column = jnp.broadcast_to(column, (depth, 128))
            for s, sign in ((0, dt), (1, -dt)):
                push = jnp.where(lane_f == face[s, x], sign * wide_column, 0.0)
                u2[c, s, x, :, :128] = u2[c, s, x, :, :128] + dt * push
                if 1 <= x <= cells:
                    vel[c, s, x - 1, :, :128] = vel[c, s, x - 1, :, :128] + push
            if 1 <= x <= cells:
                column = traction[(2 + c) * depth : (3 + c) * depth, cells - 1 + x : cells + x]
                push2[c, x - 1] = jnp.broadcast_to(dt * column, (depth, 128))

    all_of(gather1, 0).wait_send()
    all_of(gather2, 1).wait_send()


def finish_body(
    u2, d2, vel, face, push2, spec, disp_far, vel_far, dmg_far, rate, limit, hist_ref,
    disp_out, vel_out, dmg_out, hist_out,
    disp_near, vel_near, dmg_near, newest, sems,
):
    cells, depth = vel.shape[2], vel.shape[3]
    owned = newest.shape[1]
    kept = hist_ref.shape[0] - 2
    dt = time_step
    far = pl.ds(128, 128)
    near = pl.ds(0, 128)
    everything = slice(None)
    moves = [
        pltpu.make_async_copy(hist_ref.at[pl.ds(0, kept)], hist_out.at[pl.ds(2, kept)], sems.at[0]),
        pltpu.make_async_copy(disp_far, disp_out.at[:, :, :, everything, far], sems.at[1]),
        pltpu.make_async_copy(vel_far, vel_out.at[:, :, :, everything, far], sems.at[2]),
        pltpu.make_async_copy(dmg_far, dmg_out.at[:, :, everything, far], sems.at[3]),
    ]
    for copy in moves:
        copy.start()
    for step in range(2):
        lines = spec[step]
        shifted = pltpu.roll(lines, 128 - depth, 1)
        for k in range(owned):
            for ri in range(2):
                at = 2 * k + ri
                newest[step, k, ri, 0:1, :] = lines[at : at + 1, 0:depth]
                newest[step, k, ri, 1:2, :] = shifted[at : at + 1, 0:depth]
    last = pltpu.make_async_copy(newest, hist_out.at[pl.ds(0, 2)], sems.at[4])
    last.start()
    lane_f = lax.broadcasted_iota(jnp.int32, (depth, 128), 1).astype(jnp.float32)

    @pl.loop(0, cells // 2)
    def _(pair):
        for x in (2 * pair, 2 * pair + 1):
            for s in range(2):
                forces, damaged = plane(u2, d2, rate, limit, s, x, 0, depth)
                on = lane_f == face[s, x + 1]
                for c in range(2):
                    push = jnp.where(on, push2[c, x], 0.0)
                    speed = vel[c, s, x, :, half(0)] + dt * forces[c]
                    speed = speed + push if s == 0 else speed - push
                    vel_near[c, s, x] = speed
                    disp_near[c, s, x] = u2[c, s, x + 1, :, half(0)] + dt * speed
                dmg_near[s, x] = damaged
        both = pl.ds(2 * pair, 2)
        pltpu.make_async_copy(
            disp_near.at[:, :, both], disp_out.at[:, :, both, everything, near], sems.at[5]
        ).start()
        pltpu.make_async_copy(
            vel_near.at[:, :, both], vel_out.at[:, :, both, everything, near], sems.at[6]
        ).start()
        pltpu.make_async_copy(
            dmg_near.at[:, both], dmg_out.at[:, both, everything, near], sems.at[7]
        ).start()

    for copy in moves:
        copy.wait()
    last.wait()
    pltpu.make_async_copy(disp_near, disp_out.at[:, :, :, everything, near], sems.at[5]).wait()
    pltpu.make_async_copy(vel_near, vel_out.at[:, :, :, everything, near], sems.at[6]).wait()
    pltpu.make_async_copy(dmg_near, dmg_out.at[:, :, everything, near], sems.at[7]).wait()


def per_device(displacement, velocity, damage, material, damage_table, fault_rows, kernel, history):
    n = lax.axis_size("long")
    parts, strips, cells, depth, rows = displacement.shape
    length = cells * n
    owned = kernel.shape[1]
    forward, inverse = bases(length, cells)
    f32 = jnp.float32
    vmem = pl.BlockSpec(memory_space=pltpu.VMEM)
    hbm = pl.BlockSpec(memory_space=pltpu.HBM)

    def held(array):
        return pltpu.with_memory_space_constraint(array, pltpu.HBM)

    narrow = (depth, 128)
    kern = jnp.transpose(kernel, (1, 2, 3, 0))
    middle = pl.pallas_call(
        functools.partial(exchange_body, n),
        out_shape=[
            pltpu.VMEM(shape, f32)
            for shape in (
                (parts, strips, cells + 2, depth, rows),
                (strips, cells + 2, depth, rows),
                velocity.shape,
                (strips, cells + 2, *narrow),
                (parts, cells, *narrow),
                (2, cells, 128),
                (parts, strips, cells, *narrow),
                (parts, strips, cells, *narrow),
                (strips, cells, *narrow),
                damage.shape,
                damage.shape,
                history.shape,
            )
        ],
        in_specs=[hbm] * 10,
        out_specs=[vmem] * 12,
        scratch_shapes=[
            pltpu.VMEM((parts, strips, cells + 2, depth, rows), f32),
            pltpu.VMEM((strips, cells + 2, depth, rows), f32),
            pltpu.VMEM((length, 256), f32),
            pltpu.VMEM((length, 128), f32),
            pltpu.VMEM((2, length, 128), f32),
            pltpu.VMEM((6, 2 * cells, 128), f32),
            pltpu.VMEM(material.shape, material.dtype),
            pltpu.SMEM(damage_table.shape, f32),
            pltpu.VMEM(fault_rows.shape, fault_rows.dtype),
            pltpu.VMEM(kern.shape, f32),
            pltpu.VMEM(forward.shape, f32),
            pltpu.VMEM(inverse.shape, f32),
            pltpu.SemaphoreType.DMA((10,)),
            pltpu.SemaphoreType.DMA((18,)),
            pltpu.SemaphoreType.DMA((18,)),
            pltpu.SemaphoreType.DMA((2,)),
            pltpu.SemaphoreType.DMA((2,)),
        ],
        compiler_params=pltpu.CompilerParams(
            collective_id=0, has_side_effects=True, vmem_limit_bytes=40 * 1024 * 1024
        ),
    )(
        *map(held, (
            displacement, velocity, damage, material, damage_table, fault_rows, kern, history,
            jnp.asarray(forward), jnp.asarray(inverse),
        ))
    )
    return pl.pallas_call(
        finish_body,
        out_shape=tuple(
            jax.ShapeDtypeStruct(a.shape, f32) for a in (displacement, velocity, damage, history)
        ),
        in_specs=[vmem] * 12,
        out_specs=(hbm, hbm, hbm, hbm),
        scratch_shapes=[
            pltpu.VMEM((parts, strips, cells, *narrow), f32),
            pltpu.VMEM((parts, strips, cells, *narrow), f32),
            pltpu.VMEM((strips, cells, *narrow), f32),
            pltpu.VMEM((2, owned, 2, parts, depth), f32),
            pltpu.SemaphoreType.DMA((8,)),
        ],
        compiler_params=pltpu.CompilerParams(vmem_limit_bytes=24 * 1024 * 1024),
    )(*middle)


def solution(mesh):
    placed = (
        P("groups", None, "long", None, None),
        P("groups", None, "long", None, None),
        P("groups", "long", None, None),
        P("groups", "long", None, None),
        P(),
        P("groups", "long", None),
        P(None, "long", None, None),
        P("groups", "long", None, None, None),
    )
    return jax.shard_map(
        per_device,
        mesh=mesh,
        in_specs=placed,
        out_specs=(
            P("groups", None, "long", None, None),
            P("groups", None, "long", None, None),
            P("groups", "long", None, None),
            P("groups", "long", None, None, None),
        ),
        check_vma=False,
    )
```

```python
import functools
import math

import jax
import jax.numpy as jnp
import numpy as np
from jax import lax
from jax.experimental import pallas as pl
from jax.experimental.pallas import tpu as pltpu
from jax.sharding import PartitionSpec as P

time_step = 0.5
MESH = pl.DeviceIdType.MESH
HIGHEST = lax.Precision.HIGHEST


def bases(length, cells):
    waves = np.arange(length // 2)
    places = np.arange(length)
    norming = 1.0 / math.sqrt(length)

    def table(k, x):
        phase = (k[:, None] * x[None, :] % length) * (2.0 * math.pi / length)
        return np.cos(phase) * norming, -np.sin(phase) * norming

    cosine, sine = table(waves, places)
    forward = np.stack([cosine, sine], 1).reshape(length, length)
    swapped = np.stack([sine, cosine], 1).reshape(length, length)
    cosine, sine = table(waves, np.arange(-cells, length + cells))
    weights = np.where(waves == 0, 1.0, 2.0)[:, None]
    inverse = np.stack([cosine * weights, sine * weights], 1).reshape(length, -1).T
    return np.concatenate([forward, swapped], 0).astype(np.float32), inverse.astype(np.float32)


def class_lookup(material, table_ref, row):
    count = table_ref.shape[1]
    result = jnp.full(material.shape, table_ref[row, count - 1])
    for level in range(count - 1):
        result = jnp.where(material == level, table_ref[row, level], result)
    return result


def half(lanes):
    return slice(128 * lanes, 128 * lanes + 128)


def plane(u, d, rate, limit, s, x, h, depth):
    zi = lax.broadcasted_iota(jnp.int32, (depth, 128), 0)
    yi = lax.broadcasted_iota(jnp.int32, (depth, 128), 1)

    def nearby(ref, index, own_value, here):
        before, after = index
        near = [ref[(*after, slice(None), half(h))], ref[(*before, slice(None), half(h))]]
        end = here if own_value else 0.0
        near.append(jnp.where(zi == depth - 1, end, pltpu.roll(here, depth - 1, 0)))
        near.append(jnp.where(zi == 0, end, pltpu.roll(here, 1, 0)))
        middle = (*after[:-1], x + 1)
        other = ref[(*middle, slice(None), half(1 - h))]
        high, low = end, end
        if h == 0:
            high = pltpu.roll(other, 127, 1)
        else:
            low = pltpu.roll(other, 1, 1)
        near.append(jnp.where(yi == 127, high, pltpu.roll(here, 127, 1)))
        near.append(jnp.where(yi == 0, low, pltpu.roll(here, 1, 1)))
        return near

    here = d[s, x + 1, :, half(h)]
    stiff = [1.0 - 0.5 * (here + other) for other in nearby(d, ((s, x), (s, x + 2)), True, here)]
    energy = None
    forces = []
    for c in range(2):
        mid = u[c, s, x + 1, :, half(h)]
        near = nearby(u, ((c, s, x), (c, s, x + 2)), False, mid)
        force = stiff[0] * (near[0] - mid)
        for k in range(1, 6):
            force = force + stiff[k] * (near[k] - mid)
        forces.append(force)
        for k in range(3):
            slope = near[2 * k] - near[2 * k + 1]
            energy = slope * slope if energy is None else energy + slope * slope
    over = 0.25 * energy - limit[s, x, :, half(h)]
    soft = jnp.maximum(over, 0.0) + jnp.log(1.0 + jnp.exp(-jnp.abs(over)))
    kept = (1.0 - here) * jnp.exp(-rate[s, x, :, half(h)] * soft)
    return forces, 1.0 - kept


def exchange_body(
    n, disp_hbm, vel_hbm, dmg_hbm, mat_hbm, table_hbm, fault_hbm, kern_hbm, hist_hbm,
    forward_hbm, inverse_hbm,
    u2, d2, vel, face, push2, spec_out, disp_far, vel_far, dmg_far, rate, limit, hist_ref,
    u1, d1, gather1, gather2, spectra, small,
    mat_ref, table_ref, fault_ref, kern_ref, forward_ref, inverse_ref,
    load_sems, halo_send, halo_recv, all_send, all_recv,
):
    cells = vel.shape[2]
    depth = vel.shape[3]
    group = lax.axis_index("groups")
    me = lax.axis_index("long")
    left, right = lax.rem(me + n - 1, n), lax.rem(me + 1, n)
    dt = time_step

    barrier = pltpu.get_barrier_semaphore()

    @pl.loop(1, n)
    def _(step):
        pl.semaphore_signal(
            barrier, inc=1, device_id=(group, lax.rem(me + step, n)), device_id_type=MESH
        )

    loads = [
        pltpu.make_async_copy(disp_hbm, u1.at[:, :, pl.ds(1, cells)], load_sems.at[0]),
        pltpu.make_async_copy(dmg_hbm, d1.at[:, pl.ds(1, cells)], load_sems.at[1]),
        pltpu.make_async_copy(vel_hbm, vel, load_sems.at[2]),
        pltpu.make_async_copy(fault_hbm, fault_ref, load_sems.at[3]),
        pltpu.make_async_copy(kern_hbm, kern_ref, load_sems.at[4]),
        pltpu.make_async_copy(hist_hbm, hist_ref, load_sems.at[5]),
        pltpu.make_async_copy(table_hbm, table_ref, load_sems.at[6]),
        pltpu.make_async_copy(mat_hbm, mat_ref, load_sems.at[7]),
        pltpu.make_async_copy(forward_hbm, forward_ref, load_sems.at[8]),
        pltpu.make_async_copy(inverse_hbm, inverse_ref, load_sems.at[9]),
    ]
    for k in (3, 6, 0, 1, 2, 7, 4, 5, 8, 9):
        loads[k].start()
    pl.semaphore_wait(barrier, n - 1)

    def to(device, source, target, index):
        return pltpu.make_async_remote_copy(
            src_ref=source, dst_ref=target, send_sem=halo_send.at[index],
            recv_sem=halo_recv.at[index], device_id=(group, device), device_id_type=MESH,
        )

    def halo(u_from, d_from, low, u, d, h, index):
        lanes = pl.ds(128 * h, 128)
        everything = slice(None)
        high = low + cells - 1
        return [
            to(left, u_from.at[:, :, low, everything, lanes], u.at[:, :, cells + 1, everything, lanes], index),
            to(right, u_from.at[:, :, high, everything, lanes], u.at[:, :, 0, everything, lanes], index + 1),
            to(left, d_from.at[:, low, everything, lanes], d.at[:, cells + 1, everything, lanes], index + 2),
            to(right, d_from.at[:, high, everything, lanes], d.at[:, 0, everything, lanes], index + 3),
        ]

    own = pl.ds(pl.multiple_of(me * cells, cells), cells)

    def spread(buffer, index):
        @pl.loop(1, n)
        def _(step):
            pltpu.make_async_remote_copy(
                src_ref=buffer.at[own], dst_ref=buffer.at[own],
                send_sem=all_send.at[index], recv_sem=all_recv.at[index],
                device_id=(group, lax.rem(me + step, n)), device_id_type=MESH,
            ).start()

    def all_of(buffer, index):
        rest = buffer.at[pl.ds(0, (n - 1) * cells)]
        return pltpu.make_async_remote_copy(
            src_ref=rest, dst_ref=rest,
            send_sem=all_send.at[index], recv_sem=all_recv.at[index],
            device_id=(group, left), device_id_type=MESH,
        )

    faces = [
        to(left, face.at[:, 1], face.at[:, cells + 1], 16),
        to(right, face.at[:, cells], face.at[:, 0], 17),
    ]
    near1 = halo(disp_hbm, dmg_hbm, 0, u1, d1, 0, 0)
    far1 = halo(disp_hbm, dmg_hbm, 0, u1, d1, 1, 4)
    for copy in near1 + far1:
        copy.start()
    loads[3].wait()

    diagonal = lax.broadcasted_iota(jnp.int32, (depth, depth), 0) == lax.broadcasted_iota(
        jnp.int32, (depth, depth), 1
    )
    for s in range(2):
        rows_s = fault_ref[s].astype(jnp.float32)
        for x in range(cells):
            line = jnp.where(diagonal, rows_s[x : x + 1, :], 0.0)
            column = jnp.sum(line, axis=1, keepdims=True)
            face[s, x + 1] = jnp.broadcast_to(column, (depth, 128))

    lane = lax.broadcasted_iota(jnp.int32, (depth, 128), 1)
    lane_f = lane.astype(jnp.float32)
    lane8 = lax.broadcasted_iota(jnp.int32, (cells, 128), 1)

    def slip_tile(u):
        parts = []
        for c in range(2):
            total = jnp.zeros((depth, 128), jnp.float32)
            for x in range(cells):
                on0 = jnp.where(lane_f == face[0, x + 1], u[c, 0, x + 1, :, :128], 0.0)
                on1 = jnp.where(lane_f == face[1, x + 1], u[c, 1, x + 1, :, :128], 0.0)
                column = jnp.sum(on1 - on0, axis=1, keepdims=True)
                total = jnp.where(lane == x, column, total)
            parts.append(total)
        parts.append(jnp.zeros((128 - 2 * depth, 128), jnp.float32))
        return jnp.concatenate(parts, 0).T[:cells, :]

    for copy in faces:
        copy.start()
    loads[0].wait()
    loads[4].wait()
    loads[5].wait()
    owned, lags = kern_ref.shape[0], kern_ref.shape[3]
    real, imag = kern_ref[:, 0], kern_ref[:, 1]
    at_lag = [
        [jnp.broadcast_to(part[:, :, lag : lag + 1], (owned, 2, depth)) for part in (real, imag)]
        for lag in range(lags)
    ]
    zero = jnp.zeros((owned, 2, depth), jnp.float32)
    sums = [[zero, zero], [zero, zero]]
    for lag in range(1, lags):
        kr, ki = at_lag[lag]
        for step in range(2):
            if lag - 1 - step >= 0:
                now_r, now_i = hist_ref[lag - 1 - step, :, 0], hist_ref[lag - 1 - step, :, 1]
                old_r, old_i = sums[step]
                sums[step] = [old_r + kr * now_r - ki * now_i, old_i + kr * now_i + ki * now_r]
    pairs = [
        (at_lag[0][0], at_lag[0][0]), (-at_lag[0][1], at_lag[0][1]),
        (at_lag[1][0], at_lag[1][0]), (-at_lag[1][1], at_lag[1][1]),
        sums[0], sums[1],
    ]
    small[...] = jnp.zeros_like(small)
    for q, pair in enumerate(pairs):
        for ri in range(2):
            for k in range(owned):
                for c in range(2):
                    at = c * cells + 2 * k + ri
                    small[q, at : at + 1, 0:depth] = pair[ri][k, c : c + 1, :]

    def packed(q):
        second = pltpu.roll(small[q, cells : 2 * cells], depth, 1)
        return jnp.where(lane8 < depth, small[q, 0:cells], second)

    sum1, sum2 = packed(4), packed(5)
    tile = jnp.where(lane8 < 32, slip_tile(u1), pltpu.roll(sum1, 32, 1))
    tile = jnp.where(lane8 < 64, tile, pltpu.roll(sum2, 64, 1))
    for q in range(4):
        spreadable = packed(q)
        for c in range(2):
            column = spreadable[:, c * depth : c * depth + 1]
            tile = jnp.where(lane8 == 96 + 2 * q + c, column, tile)
    gather1[own, :] = jnp.where(lane8 < 104, tile, 0.0)
    spread(gather1, 0)
    for k in (1, 2, 6, 7):
        loads[k].wait()

    def first_step(s, x, h):
        material = mat_ref[s, x, :, half(h)]
        rate[s, x, :, half(h)] = class_lookup(material, table_ref, 0)
        limit[s, x, :, half(h)] = class_lookup(material, table_ref, 1)
        forces, damaged = plane(u1, d1, rate, limit, s, x, h, depth)
        for c in range(2):
            speed = vel[c, s, x, :, half(h)] + dt * forces[c]
            vel[c, s, x, :, half(h)] = speed
            u2[c, s, x + 1, :, half(h)] = u1[c, s, x + 1, :, half(h)] + dt * speed
        d2[s, x + 1, :, half(h)] = damaged

    def inner(h):
        @pl.loop(0, cells // 2 - 1)
        def _(pair):
            for x in (2 * pair + 1, 2 * pair + 2):
                for s in range(2):
                    first_step(s, x, h)

    def outer(h, arrivals):
        for copy in arrivals:
            copy.wait_recv()
        for x in (0, cells - 1):
            for s in range(2):
                first_step(s, x, h)

    inner(0)
    outer(0, near1)
    gather2[own, :] = slip_tile(u2)
    spread(gather2, 1)
    near2 = halo(u2, d2, 1, u2, d2, 0, 8)
    for copy in near2:
        copy.start()
    outer(1, far1)
    far2 = halo(u2, d2, 1, u2, d2, 1, 12)
    for copy in far2:
        copy.start()
    inner(1)

    loads[8].wait()
    loads[9].wait()
    all_of(gather1, 0).wait_recv()
    waves = forward_ref.shape[0] // 2
    terms = gather1[...]
    spec1 = jnp.dot(forward_ref[...], terms, precision=HIGHEST, preferred_element_type=jnp.float32)
    cur, cur_s = spec1[:waves], spec1[waves:]
    first_part = lax.broadcasted_iota(jnp.int32, (waves, 128), 1) < depth
    kr0, ki0, kr1, ki1 = [
        jnp.where(first_part, terms[:, at : at + 1], terms[:, at + 1 : at + 2])
        for at in (96, 98, 100, 102)
    ]
    odd = lax.broadcasted_iota(jnp.int32, (waves, 128), 0) % 2 == 1
    sums1, sums2 = pltpu.roll(terms, 96, 1), pltpu.roll(terms, 64, 1)
    sums1_s = jnp.where(odd, pltpu.roll(sums1, 1, 0), pltpu.roll(sums1, waves - 1, 0))
    tract1 = kr0 * cur + ki0 * cur_s + sums1
    tract1_s = kr0 * cur_s - ki0 * cur + sums1_s
    row = lax.broadcasted_iota(jnp.int32, (waves, 128), 0)
    wide = lax.broadcasted_iota(jnp.int32, (waves, 128), 1)
    back1 = 2.0 * dt * dt * jnp.where(row == 1, 0.0, tract1)
    back1_s = 2.0 * dt * dt * jnp.where(row == 0, 0.0, tract1_s)
    partial2 = kr1 * cur + ki1 * cur_s + sums2
    spectra[0] = cur

    for copy in near2 + far2:
        copy.wait_recv()
        copy.wait_send()

    @pl.loop(0, cells // 2)
    def _(pair):
        for x in (2 * pair, 2 * pair + 1):
            for s in range(2):
                forces, damaged = plane(u2, d2, rate, limit, s, x, 1, depth)
                for c in range(2):
                    speed = vel[c, s, x, :, half(1)] + dt * forces[c]
                    vel_far[c, s, x] = speed
                    disp_far[c, s, x] = u2[c, s, x + 1, :, half(1)] + dt * speed
                dmg_far[s, x] = damaged

    all_of(gather2, 1).wait_recv()
    spec2 = jnp.dot(
        forward_ref[...], gather2[...], precision=HIGHEST, preferred_element_type=jnp.float32
    )
    cur2 = spec2[:waves] - back1
    cur2_s = spec2[waves:] - back1_s
    spectra[1] = cur2
    tract2 = kr0 * cur2 + ki0 * cur2_s + partial2
    both = jnp.where(wide < 32, tract1, jnp.where(wide < 64, pltpu.roll(tract2, 32, 1), 0.0))
    local = inverse_ref[pl.ds(pl.multiple_of(me * cells, cells), 3 * cells), :]
    traction = lax.dot_general(
        both.T, local, (((1,), (1,)), ((), ())), precision=HIGHEST,
        preferred_element_type=jnp.float32,
    )
    spec_out[0] = spectra[1, own, :]
    spec_out[1] = spectra[0, own, :]

    for copy in faces:
        copy.wait_recv()
    for copy in faces + near1 + far1:
        copy.wait_send()

    for x in range(cells + 2):
        for c in range(2):
            column = traction[c * depth : (c + 1) * depth, cells - 1 + x : cells + x]
            wide_column = jnp.broadcast_to(column, (depth, 128))
            for s, sign in ((0, dt), (1, -dt)):
                push = jnp.where(lane_f == face[s, x], sign * wide_column, 0.0)
                u2[c, s, x, :, :128] = u2[c, s, x, :, :128] + dt * push
                if 1 <= x <= cells:
                    vel[c, s, x - 1, :, :128] = vel[c, s, x - 1, :, :128] + push
            if 1 <= x <= cells:
                column = traction[(2 + c) * depth : (3 + c) * depth, cells - 1 + x : cells + x]
                push2[c, x - 1] = jnp.broadcast_to(dt * column, (depth, 128))

    all_of(gather1, 0).wait_send()
    all_of(gather2, 1).wait_send()


def finish_body(
    u2, d2, vel, face, push2, spec, disp_far, vel_far, dmg_far, rate, limit, hist_ref,
    disp_out, vel_out, dmg_out, hist_out,
    disp_near, vel_near, dmg_near, newest, sems,
):
    cells, depth = vel.shape[2], vel.shape[3]
    owned = newest.shape[1]
    kept = hist_ref.shape[0] - 2
    dt = time_step
    far = pl.ds(128, 128)
    near = pl.ds(0, 128)
    everything = slice(None)
    moves = [
        pltpu.make_async_copy(hist_ref.at[pl.ds(0, kept)], hist_out.at[pl.ds(2, kept)], sems.at[0]),
        pltpu.make_async_copy(disp_far, disp_out.at[:, :, :, everything, far], sems.at[1]),
        pltpu.make_async_copy(vel_far, vel_out.at[:, :, :, everything, far], sems.at[2]),
        pltpu.make_async_copy(dmg_far, dmg_out.at[:, :, everything, far], sems.at[3]),
    ]
    for copy in moves:
        copy.start()
    for step in range(2):
        lines = spec[step]
        shifted = pltpu.roll(lines, 128 - depth, 1)
        for k in range(owned):
            for ri in range(2):
                at = 2 * k + ri
                newest[step, k, ri, 0:1, :] = lines[at : at + 1, 0:depth]
                newest[step, k, ri, 1:2, :] = shifted[at : at + 1, 0:depth]
    last = pltpu.make_async_copy(newest, hist_out.at[pl.ds(0, 2)], sems.at[4])
    last.start()
    lane_f = lax.broadcasted_iota(jnp.int32, (depth, 128), 1).astype(jnp.float32)

    @pl.loop(0, cells // 2)
    def _(pair):
        for x in (2 * pair, 2 * pair + 1):
            for s in range(2):
                forces, damaged = plane(u2, d2, rate, limit, s, x, 0, depth)
                on = lane_f == face[s, x + 1]
                for c in range(2):
                    push = jnp.where(on, push2[c, x], 0.0)
                    speed = vel[c, s, x, :, half(0)] + dt * forces[c]
                    speed = speed + push if s == 0 else speed - push
                    vel_near[c, s, x] = speed
                    disp_near[c, s, x] = u2[c, s, x + 1, :, half(0)] + dt * speed
                dmg_near[s, x] = damaged
        both = pl.ds(2 * pair, 2)
        pltpu.make_async_copy(
            disp_near.at[:, :, both], disp_out.at[:, :, both, everything, near], sems.at[5]
        ).start()
        pltpu.make_async_copy(
            vel_near.at[:, :, both], vel_out.at[:, :, both, everything, near], sems.at[6]
        ).start()
        pltpu.make_async_copy(
            dmg_near.at[:, both], dmg_out.at[:, both, everything, near], sems.at[7]
        ).start()

    for copy in moves:
        copy.wait()
    last.wait()
    pltpu.make_async_copy(disp_near, disp_out.at[:, :, :, everything, near], sems.at[5]).wait()
    pltpu.make_async_copy(vel_near, vel_out.at[:, :, :, everything, near], sems.at[6]).wait()
    pltpu.make_async_copy(dmg_near, dmg_out.at[:, :, everything, near], sems.at[7]).wait()


def per_device(displacement, velocity, damage, material, damage_table, fault_rows, kernel, history):
    n = lax.axis_size("long")
    parts, strips, cells, depth, rows = displacement.shape
    length = cells * n
    owned = kernel.shape[1]
    forward, inverse = bases(length, cells)
    f32 = jnp.float32
    vmem = pl.BlockSpec(memory_space=pltpu.VMEM)
    hbm = pl.BlockSpec(memory_space=pltpu.HBM)

    def held(array):
        return pltpu.with_memory_space_constraint(array, pltpu.HBM)

    narrow = (depth, 128)
    kern = jnp.transpose(kernel, (1, 2, 3, 0))
    middle = pl.pallas_call(
        functools.partial(exchange_body, n),
        out_shape=[
            pltpu.VMEM(shape, f32)
            for shape in (
                (parts, strips, cells + 2, depth, rows),
                (strips, cells + 2, depth, rows),
                velocity.shape,
                (strips, cells + 2, *narrow),
                (parts, cells, *narrow),
                (2, cells, 128),
                (parts, strips, cells, *narrow),
                (parts, strips, cells, *narrow),
                (strips, cells, *narrow),
                damage.shape,
                damage.shape,
                history.shape,
            )
        ],
        in_specs=[hbm] * 10,
        out_specs=[vmem] * 12,
        scratch_shapes=[
            pltpu.VMEM((parts, strips, cells + 2, depth, rows), f32),
            pltpu.VMEM((strips, cells + 2, depth, rows), f32),
            pltpu.VMEM((length, 128), f32),
            pltpu.VMEM((length, 128), f32),
            pltpu.VMEM((2, length, 128), f32),
            pltpu.VMEM((6, 2 * cells, 128), f32),
            pltpu.VMEM(material.shape, material.dtype),
            pltpu.SMEM(damage_table.shape, f32),
            pltpu.VMEM(fault_rows.shape, fault_rows.dtype),
            pltpu.VMEM(kern.shape, f32),
            pltpu.VMEM(forward.shape, f32),
            pltpu.VMEM(inverse.shape, f32),
            pltpu.SemaphoreType.DMA((10,)),
            pltpu.SemaphoreType.DMA((18,)),
            pltpu.SemaphoreType.DMA((18,)),
            pltpu.SemaphoreType.DMA((2,)),
            pltpu.SemaphoreType.DMA((2,)),
        ],
        compiler_params=pltpu.CompilerParams(
            collective_id=0, has_side_effects=True, vmem_limit_bytes=40 * 1024 * 1024
        ),
    )(
        *map(held, (
            displacement, velocity, damage, material, damage_table, fault_rows, kern, history,
            jnp.asarray(forward), jnp.asarray(inverse),
        ))
    )
    return pl.pallas_call(
        finish_body,
        out_shape=tuple(
            jax.ShapeDtypeStruct(a.shape, f32) for a in (displacement, velocity, damage, history)
        ),
        in_specs=[vmem] * 12,
        out_specs=(hbm, hbm, hbm, hbm),
        scratch_shapes=[
            pltpu.VMEM((parts, strips, cells, *narrow), f32),
            pltpu.VMEM((parts, strips, cells, *narrow), f32),
            pltpu.VMEM((strips, cells, *narrow), f32),
            pltpu.VMEM((2, owned, 2, parts, depth), f32),
            pltpu.SemaphoreType.DMA((8,)),
        ],
        compiler_params=pltpu.CompilerParams(vmem_limit_bytes=24 * 1024 * 1024),
    )(*middle)


def solution(mesh):
    placed = (
        P("groups", None, "long", None, None),
        P("groups", None, "long", None, None),
        P("groups", "long", None, None),
        P("groups", "long", None, None),
        P(),
        P("groups", "long", None),
        P(None, "long", None, None),
        P("groups", "long", None, None, None),
    )
    return jax.shard_map(
        per_device,
        mesh=mesh,
        in_specs=placed,
        out_specs=(
            P("groups", None, "long", None, None),
            P("groups", None, "long", None, None),
            P("groups", "long", None, None),
            P("groups", "long", None, None, None),
        ),
        check_vma=False,
    )
```
